256 devices in a mesh: vertex: 16 (over z, core), tm: 16 (over y, x).
Axes of the slice: x: 4, y: 4, z: 8, core: 2. Of those that a mesh axis runs over, the one named last changes fastest.
Arguments:
- features: bfloat16 [16, 16384, 512], P('tm', 'vertex'), may hold values from -6 to 6
- tile_coord: int32 [16, 2048, 2], P('tm', 'vertex'), may hold values from 0 to 127, as said below
- tile_count: int32 [16, 16], P('tm', 'vertex'), may hold values from 1 to 128, as said below
- tile_values: bfloat16 [16, 2048, 128, 128], P('tm', 'vertex'), may hold values from -0.125 to 0.125
- w_agg: bfloat16 [512, 512], replicated, may hold values from -0.25 to 0.25
- w_root: bfloat16 [512, 512], replicated, may hold values from -0.25 to 0.25
- time_embed: bfloat16 [16, 512], replicated, may hold values from -6 to 6
- gain_first: bfloat16 [512], replicated, may hold values from 0.25 to 1.75
- w_qkv: bfloat16 [512, 1536], replicated, may hold values from -12 to 12
- w_out: bfloat16 [512, 512], replicated, may hold values from -0.25 to 0.25
- gain_second: bfloat16 [512], replicated, may hold values from 0.25 to 1.75
- w_up: bfloat16 [512, 1024], replicated, may hold values from -0.25 to 0.25
- w_down: bfloat16 [1024, 512], replicated, may hold values from -0.1875 to 0.1875
Outputs:
- layer_out: bfloat16 [16, 16384, 512], P(None, ('vertex', 'tm'))
The draws below stay inside these ranges and needn't reach their ends.
Inputs may be any that keep to these rules, and one draw needn't show every extreme that they name: `tile_coord`: entry 0 of a slot is a row block 0 to 7 of the device's own vertices, entry 1 a column block 0 to 127; no pair repeats among one device's 128 slots, live or not. `tile_count`: live slots are the first ones of a device; in every snapshot some device has all 128 slots live.
All inputs are finite; a program needn't handle non-finite values.
Results may differ from the reference program's by a relative error of at most 0.006.
Values may be sent and summed in bfloat16 or wider, within the bound.
No kernel may reach another device: no remote copies, remote signals or barrier semaphores. Data moves between devices by JAX's collectives and lax.ppermute only.
A program may use at most 192 MiB of HBM per device.

```python
import math
import jax
import jax.numpy as jnp
from jax import lax

D = 512
HID = 1024
HEADS = 8
TILE = 128
TILE_ROW = 16
VB = 1024
TILES_DEV = 128
NV = 16384
SNAPS = 16
N_VERTEX = 16


def draw_tile_coord(key, part):
    group_count = NV // VB
    row_blocks = VB // TILE
    col_blocks = NV // TILE
    device_keys = jax.random.split(key, SNAPS * group_count)

    def one_device(device_key):
        shuffled = jax.random.permutation(device_key, row_blocks * col_blocks)[:TILES_DEV]
        return jnp.stack([shuffled // col_blocks, shuffled % col_blocks], axis=-1)
    pair_rows = jax.vmap(one_device)(device_keys)
    return pair_rows.reshape(SNAPS, group_count * TILES_DEV, 2).astype(jnp.int32)


def draw_tile_count(key, part):
    group_count = NV // VB
    key_first, key_second = jax.random.split(jax.random.fold_in(key, 7))
    counts = jax.random.randint(key_first, (SNAPS, group_count), 1, TILES_DEV + 1)
    full_index = jax.random.randint(key_second, (SNAPS, 1), 0, group_count)
    filled = jnp.where(jnp.arange(group_count)[None, :] == full_index, TILES_DEV, counts)
    return filled.astype(jnp.int32)


def draw_w_qkv(key, part):
    key_first = jax.random.fold_in(jax.random.fold_in(key, 11), 0)
    base = jax.random.normal(key_first, (D, 3 * D), jnp.float32) / math.sqrt(D)
    return base.astype(jnp.bfloat16)


def shard_levels(stream_key, shape, shards, smallest, high):
    loudness = 1.0
    for axis_at, parts in shards:
        heights = jax.random.uniform(jax.random.fold_in(jax.random.fold_in(stream_key, 6), axis_at), (parts,), jnp.float32, smallest / len(shards), high / len(shards))
        loudness = loudness * jnp.repeat(jnp.exp(heights), shape[axis_at] // parts).reshape((-1,) + (1,) * (len(shape) - 1 - axis_at))
    return loudness


def scatter_about(key, dims, deviation, bound, cuts=(), dtype=jnp.bfloat16):
    factor_of = shard_levels(key, dims, cuts, -0.22, 0.18) if cuts else 1.0
    array = jax.random.normal(key, dims, jnp.float32) * deviation * factor_of
    return jnp.minimum(jnp.maximum(array, -bound), bound).astype(dtype)


def setup_inputs(seed: int = 0) -> dict:
    splits = jax.random.split(jax.random.key(seed), 14)
    features = scatter_about(splits[0], (SNAPS, NV, D), 1.0, 6.0, ((0, 16), (1, 16)))
    tile_coord = draw_tile_coord(jax.random.fold_in(splits[13], 71), 0)
    tile_count = draw_tile_count(jax.random.fold_in(splits[13], 71), 0)
    tile_values = scatter_about(splits[3], (SNAPS, N_VERTEX * TILES_DEV, TILE, TILE), (TILE * TILE_ROW) ** -0.5, 0.125, ((0, 16), (1, 16)))
    w_agg = scatter_about(splits[4], (D, D), D ** -0.5, 0.25)
    w_root = scatter_about(splits[5], (D, D), D ** -0.5, 0.25)
    time_embed = scatter_about(splits[6], (SNAPS, D), 1.0, 6.0)
    gain_first = jnp.clip(1.0 + 0.15 * jax.random.normal(splits[7], (D,), jnp.float32), 0.25, 1.75).astype(jnp.bfloat16)
    w_qkv = draw_w_qkv(jax.random.fold_in(splits[13], 71), 0)
    w_out = scatter_about(splits[9], (D, D), D ** -0.5, 0.25)
    gain_second = jnp.clip(1.0 + 0.15 * jax.random.normal(splits[10], (D,), jnp.float32), 0.25, 1.75).astype(jnp.bfloat16)
    w_up = scatter_about(splits[11], (D, HID), D ** -0.5, 0.25)
    w_down = scatter_about(splits[12], (HID, D), HID ** -0.5, 0.1875)
    return dict(features=features, tile_coord=tile_coord, tile_count=tile_count, tile_values=tile_values, w_agg=w_agg, w_root=w_root, time_embed=time_embed, gain_first=gain_first, w_qkv=w_qkv, w_out=w_out, gain_second=gain_second, w_up=w_up, w_down=w_down)


def norm_rows(values, gain):
    scale = lax.rsqrt(lax.optimization_barrier(jnp.mean(values * values, axis=-1, keepdims=True)) + 1e-06)
    return values * scale * gain.astype(jnp.float32)

def project(left, right):
    return jnp.einsum('sid,de->sie', left.astype(jnp.float32), right.astype(jnp.float32))

def temporal(graph_rows, time_embed, gain_first, w_qkv, w_out, gain_second, w_up, w_down):
    snap_count, item_count, width = graph_rows.shape
    head_size = width // HEADS
    mixed = graph_rows.astype(jnp.float32) + time_embed.astype(jnp.float32)[:, None, :]
    normed = norm_rows(mixed, gain_first).astype(jnp.bfloat16)
    qkv = project(normed, w_qkv).astype(jnp.bfloat16)
    query = qkv[..., :width].reshape(snap_count, item_count, HEADS, head_size).astype(jnp.float32)
    key_rows = qkv[..., width:2 * width].reshape(snap_count, item_count, HEADS, head_size).astype(jnp.float32)
    value_rows = qkv[..., 2 * width:].reshape(snap_count, item_count, HEADS, head_size).astype(jnp.float32)
    scores = jnp.einsum('sihd,tihd->ihst', query, key_rows) / math.sqrt(head_size)
    causal = jnp.arange(snap_count)[:, None] >= jnp.arange(snap_count)[None, :]
    scores = jnp.where(causal, scores, -1e+30)
    largest = lax.optimization_barrier(jnp.max(scores, axis=-1, keepdims=True))
    expo = jnp.where(causal, jnp.exp(scores - largest), 0.0)
    weights_soft = (expo / lax.optimization_barrier(jnp.sum(expo, axis=-1, keepdims=True))).astype(jnp.bfloat16)
    context = jnp.einsum('ihst,tihd->sihd', weights_soft.astype(jnp.float32), value_rows)
    context = context.astype(jnp.bfloat16).reshape(snap_count, item_count, width)
    residual = mixed + project(context, w_out)
    normed_two = norm_rows(residual, gain_second).astype(jnp.bfloat16)
    hidden = jax.nn.gelu(project(normed_two, w_up)).astype(jnp.bfloat16)
    return (residual + project(hidden, w_down)).astype(jnp.bfloat16)

def reference(features, tile_coord, tile_count, tile_values, w_agg, w_root, time_embed, gain_first, w_qkv, w_out, gain_second, w_up, w_down):
    snap_count, vertex_count, width = features.shape
    row_blocks = VB // TILE
    col_blocks = vertex_count // TILE
    group_count = vertex_count // VB
    slot_index = jnp.arange(group_count * TILES_DEV)
    owner_index = slot_index // TILES_DEV
    local_slot = slot_index % TILES_DEV

    def one_snapshot(packed):
        own_rows, tile_pairs, live_count, tile_block = packed
        blocks = own_rows.reshape(col_blocks, TILE, width)
        chosen = blocks[tile_pairs[:, 1]]
        products = jnp.einsum('tij,tjd->tid', tile_block.astype(jnp.float32), chosen.astype(jnp.float32))
        alive = (local_slot < live_count[owner_index]).astype(jnp.float32)
        products = products * alive[:, None, None]
        target = (owner_index * row_blocks + tile_pairs[:, 0]).astype(jnp.int32)
        summed = jax.ops.segment_sum(products, target, num_segments=col_blocks)
        neighbor_sum = summed.reshape(vertex_count, width).astype(jnp.bfloat16)
        combined = jnp.dot(neighbor_sum, w_agg, preferred_element_type=jnp.float32)
        combined = combined + jnp.dot(own_rows, w_root, preferred_element_type=jnp.float32)
        return jax.nn.gelu(combined).astype(jnp.bfloat16)
    graph_rows = lax.map(one_snapshot, (features, tile_coord, tile_count, tile_values))
    grouped = graph_rows.reshape(snap_count, group_count, VB, width).transpose(1, 0, 2, 3)

    def one_group(rows):
        return temporal(rows, time_embed, gain_first, w_qkv, w_out, gain_second, w_up, w_down)
    mixed_out = lax.map(one_group, grouped)
    return mixed_out.transpose(1, 0, 2, 3).reshape(snap_count, vertex_count, width)
```

```python
import functools

import jax
import jax.numpy as jnp
from jax import lax
from jax.experimental import pallas as pl
from jax.experimental.pallas import tpu as pltpu
from jax.sharding import PartitionSpec as P

TILE = 128
WIDTH = 512
LOCAL = 1024
SLOTS = 128
ROWS = LOCAL // TILE
HALF = LOCAL // 2
STAGES = ((0, 1, 7), (2, 6), (3, 5), (4,))
ITEMS = 32


def products_kernel(n_bufs, stage, first, last, *refs):
    slot_ref, block_ref, offset_ref = refs[:3]
    refs = refs[3:]
    acc_in = None
    if not first:
        acc_in, refs = refs[0], refs[1:]
    tiles, bufs, refs = refs[0], refs[1 : 1 + n_bufs], refs[1 + n_bufs :]
    if last:
        own_ref, agg_ref, root_ref, out_ref, acc, tile_buf, feat_buf, tile_sem, feat_sem = refs
    else:
        acc, tile_buf, feat_buf, tile_sem, feat_sem = refs
    begin, end = offset_ref[stage * ROWS], offset_ref[(stage + 1) * ROWS]

    start = 0
    feature_copies = []
    for k, buf in enumerate(bufs):
        copy = pltpu.make_async_copy(
            buf, feat_buf.at[pl.ds(start, buf.shape[0])], feat_sem.at[k]
        )
        copy.start()
        feature_copies.append(copy)
        start += buf.shape[0]

    @pl.loop(begin, end)
    def _(p):
        pltpu.make_async_copy(tiles.at[slot_ref[p]], tile_buf.at[p], tile_sem.at[p]).start()

    tile_buf[SLOTS] = jnp.zeros((TILE, TILE), jnp.bfloat16)
    if first:
        acc[...] = jnp.zeros_like(acc)
    else:
        acc[...] = acc_in[...]
    for copy in feature_copies:
        copy.wait()

    @pl.loop(begin, end)
    def _(p):
        pltpu.make_async_copy(tiles.at[0], tile_buf.at[p], tile_sem.at[p]).wait()

    @pl.loop(0, ROWS)
    def _(row):
        low, high = offset_ref[stage * ROWS + row], offset_ref[stage * ROWS + row + 1]
        rows = pl.ds(pl.multiple_of(row * TILE, TILE), TILE)

        @pl.loop(0, (high - low + 1) // 2)
        def _(pair):
            p0 = low + 2 * pair
            p1 = jnp.where(p0 + 1 < high, p0 + 1, SLOTS)
            q1 = jnp.minimum(p0 + 1, high - 1)
            f0 = pl.ds(pl.multiple_of(block_ref[p0] * TILE, TILE), TILE)
            f1 = pl.ds(pl.multiple_of(block_ref[q1] * TILE, TILE), TILE)
            left = jnp.concatenate([tile_buf[p0], tile_buf[p1]], axis=1)
            right = jnp.concatenate([feat_buf[f0, :], feat_buf[f1, :]], axis=0)
            acc[rows, :] += jnp.dot(left, right, preferred_element_type=jnp.float32)

    if last:

        @pl.loop(0, 4)
        def _(i):
            rows = pl.ds(pl.multiple_of(i * 256, 256), 256)
            combined = jnp.dot(
                acc[rows, :].astype(jnp.bfloat16),
                agg_ref[...],
                preferred_element_type=jnp.float32,
            )
            combined += jnp.dot(
                own_ref[rows, :], root_ref[...], preferred_element_type=jnp.float32
            )
            out_ref[rows, :] = jax.nn.gelu(combined).astype(jnp.bfloat16)


def products(stage, scalars, acc, tiles, bufs, tail=None):
    first, last = acc is None, tail is not None
    n_rows = sum(b.shape[0] for b in bufs)
    smem = pl.BlockSpec(memory_space=pltpu.SMEM)
    vmem = pl.BlockSpec(memory_space=pltpu.VMEM)
    anywhere = pl.BlockSpec(memory_space=pl.ANY)
    args, specs = list(scalars), [smem] * 3
    if not first:
        args.append(acc)
        specs.append(vmem)
    args += [tiles, *bufs]
    specs += [anywhere] * (1 + len(bufs))
    scratch = [
        pltpu.VMEM((SLOTS + 1, TILE, TILE), jnp.bfloat16),
        pltpu.VMEM((n_rows, WIDTH), jnp.bfloat16),
        pltpu.SemaphoreType.DMA((SLOTS,)),
        pltpu.SemaphoreType.DMA((len(bufs),)),
    ]
    if last:
        args += list(tail)
        specs += [vmem] * len(tail)
        scratch = [pltpu.VMEM((LOCAL, WIDTH), jnp.float32), *scratch]
        out = jax.ShapeDtypeStruct((LOCAL, WIDTH), jnp.bfloat16)
    else:
        out = jax.ShapeDtypeStruct((LOCAL, WIDTH), jnp.float32)
    flops = 2 * LOCAL * n_rows * WIDTH // 4
    return pl.pallas_call(
        functools.partial(products_kernel, len(bufs), stage, first, last),
        out_shape=out,
        in_specs=specs,
        out_specs=vmem,
        scratch_shapes=scratch,
        compiler_params=pltpu.CompilerParams(vmem_limit_bytes=24 << 20),
        cost_estimate=pl.CostEstimate(
            flops=flops, bytes_accessed=n_rows * WIDTH * 2 + (8 << 20), transcendentals=0
        ),
        name=f"products_{stage}",
    )(*args)


def norm_rows(values, gain):
    scale = lax.rsqrt(jnp.mean(values * values, axis=-1, keepdims=True) + 1e-06)
    return (values * scale * gain).astype(jnp.bfloat16)


def temporal_kernel(
    rows_ref, embed_ref, gain1_ref, qkv_ref, out_w_ref, gain2_ref, up_ref, down_ref, out_ref
):
    groups = ITEMS // 8
    embed = embed_ref[...].astype(jnp.float32)
    embed = jnp.broadcast_to(embed[:, None, :], (16, 8, WIDTH)).reshape(TILE, WIDTH)
    values = rows_ref[...].astype(jnp.float32)
    mixed = jnp.concatenate(
        [values[:, g * 8 : (g + 1) * 8, :].reshape(TILE, WIDTH) + embed for g in range(groups)],
        axis=0,
    )
    normed = norm_rows(mixed, gain1_ref[...].astype(jnp.float32))
    qkv = jnp.dot(normed, qkv_ref[...], preferred_element_type=jnp.float32).astype(jnp.bfloat16)

    at = lax.broadcasted_iota(jnp.int32, (2 * TILE, TILE), 0) % TILE
    to = lax.broadcasted_iota(jnp.int32, (2 * TILE, TILE), 1)
    allowed = (at % 8 == to % 8) & (to // 8 <= at // 8)
    lane = lax.broadcasted_iota(jnp.int32, (TILE, TILE), 1)
    low_half = lane < 64
    zero = jnp.zeros((TILE, TILE), jnp.bfloat16)
    contexts = []
    for g in range(groups):
        rows = slice(g * TILE, (g + 1) * TILE)
        pieces = []
        for pair in range(4):
            cols = slice(pair * TILE, (pair + 1) * TILE)
            query = qkv[rows, pair * TILE : (pair + 1) * TILE] * jnp.bfloat16(0.125)
            key = qkv[rows, WIDTH + pair * TILE : WIDTH + (pair + 1) * TILE]
            value = qkv[rows, 2 * WIDTH + pair * TILE : 2 * WIDTH + (pair + 1) * TILE]
            split_query = jnp.concatenate(
                [jnp.where(low_half, query, zero), jnp.where(low_half, zero, query)], axis=0
            )
            split_value = jnp.concatenate(
                [jnp.where(low_half, value, zero), jnp.where(low_half, zero, value)], axis=0
            )
            scores = lax.dot_general(
                split_query, key, (((1,), (1,)), ((), ())), preferred_element_type=jnp.float32
            )
            scores = jnp.where(allowed, scores, -1e30)
            expo = jnp.exp(scores - jnp.max(scores, axis=-1, keepdims=True))
            weights = (expo / jnp.sum(expo, axis=-1, keepdims=True)).astype(jnp.bfloat16)
            both = jnp.concatenate([weights[:TILE], weights[TILE:]], axis=1)
            pieces.append(jnp.dot(both, split_value, preferred_element_type=jnp.float32))
        contexts.append(jnp.concatenate(pieces, axis=1))
    context = jnp.concatenate(contexts, axis=0).astype(jnp.bfloat16)
    residual = mixed + jnp.dot(context, out_w_ref[...], preferred_element_type=jnp.float32)
    normed_two = norm_rows(residual, gain2_ref[...].astype(jnp.float32))
    hidden = jax.nn.gelu(
        jnp.dot(normed_two, up_ref[...], preferred_element_type=jnp.float32)
    ).astype(jnp.bfloat16)
    result = residual + jnp.dot(hidden, down_ref[...], preferred_element_type=jnp.float32)
    for g in range(groups):
        piece = result[g * TILE : (g + 1) * TILE].reshape(16, 8, WIDTH)
        out_ref[:, g * 8 : (g + 1) * 8, :] = piece.astype(jnp.bfloat16)


def temporal(rows, embed, gain1, w_qkv, w_out, gain2, w_up, w_down):
    snaps, items, width = rows.shape

    def whole(array):
        return pl.BlockSpec(array.shape, lambda i: (0,) * array.ndim, pipeline_mode=pl.Buffered(1))

    block = pl.BlockSpec((snaps, ITEMS, width), lambda i: (0, i, 0))
    weights = (embed, gain1[None, :], w_qkv, w_out, gain2[None, :], w_up, w_down)
    return pl.pallas_call(
        temporal_kernel,
        grid=(items // ITEMS,),
        out_shape=jax.ShapeDtypeStruct(rows.shape, jnp.bfloat16),
        in_specs=[block] + [whole(w) for w in weights],
        out_specs=block,
        compiler_params=pltpu.CompilerParams(vmem_limit_bytes=40 << 20),
        name="temporal",
    )(rows, *weights)


def plan(pairs, count, vertex):
    row, col = pairs[:, 0], pairs[:, 1]
    shard = col // 8
    block = col % 8
    distance = (vertex // 2 - shard // 2) % 8
    other = (shard % 2) ^ (vertex % 2)
    stage_of, place_of = [0] * 8, [0] * 8
    for s, distances in enumerate(STAGES):
        for i, d in enumerate(distances):
            stage_of[d], place_of[d] = s, i
    stage = sum(jnp.where(distance == d, stage_of[d], 0) for d in range(8))
    place = sum(jnp.where(distance == d, place_of[d], 0) for d in range(8))
    where = (place * 2 + other) * 8 + block
    index = jnp.arange(SLOTS, dtype=jnp.int32)
    n_keys = len(STAGES) * ROWS
    key = jnp.where(index < count, stage * ROWS + row, n_keys)
    before = (key[None, :] < key[:, None]) | (
        (key[None, :] == key[:, None]) & (index[None, :] < index[:, None])
    )
    rank = jnp.sum(before.astype(jnp.int32), axis=1)
    hit = rank[None, :] == index[:, None]
    slots = jnp.sum(jnp.where(hit, index[None, :], 0), axis=1)
    blocks = jnp.sum(jnp.where(hit, where[None, :], 0), axis=1)
    bounds = jnp.arange(n_keys + 1, dtype=jnp.int32)
    offsets = jnp.sum((key[None, :] < bounds[:, None]).astype(jnp.int32), axis=1)
    return slots, blocks, offsets


def per_device(
    features,
    tile_coord,
    tile_count,
    tile_values,
    w_agg,
    w_root,
    time_embed,
    gain_first,
    w_qkv,
    w_out,
    gain_second,
    w_up,
    w_down,
):
    own = features[0]
    tiles = tile_values[0]
    n_vertex = lax.axis_size("vertex")

    def hop(x, step):
        return lax.ppermute(
            x, "vertex", [(v, (v + 2 * step) % n_vertex) for v in range(n_vertex)]
        )

    def swap(x):
        return lax.ppermute(x, "vertex", [(v, v ^ 1) for v in range(n_vertex)])

    chunks = (own[:HALF], own[HALF:])
    got = {0: (own, swap(own))}
    right, left = list(chunks), list(chunks)
    for h in (1, 2, 3):
        for c in (0, 1):
            right[c], left[c] = hop(right[c], 1), hop(left[c], -1)
        got[h] = (right[0], right[1], swap(right[0]), swap(right[1]))
        got[8 - h] = (left[0], left[1], swap(left[0]), swap(left[1]))
    far = (hop(right[0], 1), hop(left[1], -1))
    got[4] = (far[0], far[1], swap(far[0]), swap(far[1]))

    scalars = plan(tile_coord[0], tile_count[0, 0], lax.axis_index("vertex"))
    acc = None
    for s, distances in enumerate(STAGES):
        bufs = [b for d in distances for b in got[d]]
        tail = (own, w_agg, w_root) if s == len(STAGES) - 1 else None
        acc = products(s, scalars, acc, tiles, bufs, tail)
    tm_count = lax.axis_size("tm")
    sections = acc.reshape(tm_count, LOCAL // tm_count, WIDTH)
    arrived = lax.all_to_all(sections, "tm", split_axis=0, concat_axis=0, tiled=True)
    return temporal(arrived, time_embed, gain_first, w_qkv, w_out, gain_second, w_up, w_down)


def solution(mesh):
    return jax.shard_map(
        per_device,
        mesh=mesh,
        in_specs=(
            P("tm", "vertex", None),
            P("tm", "vertex", None),
            P("tm", "vertex"),
            P("tm", "vertex", None, None),
            P(),
            P(),
            P(),
            P(),
            P(),
            P(),
            P(),
            P(),
            P(),
        ),
        out_specs=P(None, ("vertex", "tm"), None),
        check_vma=False,
    )
```

```python
import functools

import jax
import jax.numpy as jnp
from jax import lax
from jax.experimental import pallas as pl
from jax.experimental.pallas import tpu as pltpu
from jax.sharding import PartitionSpec as P


TILE = 128
WIDTH = 512
LOCAL = 1024
SLOTS = 128
ROWS = LOCAL // TILE
HALF = LOCAL // 2
STAGES = ((0,), (1, 7), (2, 6), (3, 5), (4,))
PAIRS = 72
UNROLL = 4
ITEMS = 32


def products_kernel(n_bufs, stage, first, last, *refs):
    left_ref, right_ref, count_ref = refs[:3]
    refs = refs[3:]
    if first:
        own_ref, root_ref, refs = refs[0], refs[1], refs[2:]
    else:
        acc_in, refs = refs[0], refs[1:]
    if last:
        base_ref, agg_ref, refs = refs[0], refs[1], refs[2:]
    tiles, bufs, refs = refs[0], refs[1 : 1 + n_bufs], refs[1 + n_bufs :]
    if first:
        acc, base_out, feat_buf, feat_sem = refs
    elif last:
        out_ref, acc, feat_buf, feat_sem = refs
    else:
        acc, feat_buf, feat_sem = refs

    start = 0
    feature_copies = []
    for k, buf in enumerate(bufs):
        copy = pltpu.make_async_copy(
            buf, feat_buf.at[pl.ds(start, buf.shape[0])], feat_sem.at[k]
        )
        copy.start()
        feature_copies.append(copy)
        start += buf.shape[0]
    if first:
        acc[...] = jnp.zeros_like(acc)
    else:
        acc[...] = acc_in[...]
    for copy in feature_copies:
        copy.wait()

    def half(code):
        tile = tiles[code & 127]
        live = (code >> 13) & 1
        tile = jnp.where(live == 1, tile, jnp.zeros_like(tile))
        block = pl.multiple_of(((code >> 7) & 63) * TILE, TILE)
        return tile, feat_buf[pl.ds(block, TILE), :]

    @pl.loop(0, (count_ref[stage] + UNROLL - 1) // UNROLL)
    def _(step):
        for u in range(UNROLL):
            at = stage * PAIRS + step * UNROLL + u
            code = left_ref[at]
            tile0, feat0 = half(code)
            tile1, feat1 = half(right_ref[at])
            product = jnp.dot(
                jnp.concatenate([tile0, tile1], axis=1),
                jnp.concatenate([feat0, feat1], axis=0),
                preferred_element_type=jnp.float32,
            )
            rows = pl.ds(pl.multiple_of((code >> 14) * TILE, TILE), TILE)
            acc[rows, :] += product

    if first:

        @pl.loop(0, 4)
        def _(i):
            rows = pl.ds(pl.multiple_of(i * 256, 256), 256)
            base_out[rows, :] = jnp.dot(
                own_ref[rows, :], root_ref[...], preferred_element_type=jnp.float32
            )

    if last:

        @pl.loop(0, 4)
        def _(i):
            rows = pl.ds(pl.multiple_of(i * 256, 256), 256)
            combined = base_ref[rows, :] + jnp.dot(
                acc[rows, :].astype(jnp.bfloat16),
                agg_ref[...],
                preferred_element_type=jnp.float32,
            )
            out_ref[rows, :] = jax.nn.gelu(combined).astype(jnp.bfloat16)


def products(stage, scalars, extra, tiles, bufs, first=False, last=False):
    n_rows = sum(b.shape[0] for b in bufs)
    smem = pl.BlockSpec(memory_space=pltpu.SMEM)
    vmem = pl.BlockSpec(memory_space=pltpu.VMEM)
    anywhere = pl.BlockSpec(memory_space=pl.ANY)
    scratch = [
        pltpu.VMEM((n_rows, WIDTH), jnp.bfloat16),
        pltpu.SemaphoreType.DMA((len(bufs),)),
    ]
    partial = jax.ShapeDtypeStruct((LOCAL, WIDTH), jnp.float32)
    out, out_specs = partial, vmem
    if first:
        out, out_specs = (partial, partial), (vmem, vmem)
    if last:
        scratch = [pltpu.VMEM((LOCAL, WIDTH), jnp.float32), *scratch]
        out = jax.ShapeDtypeStruct((LOCAL, WIDTH), jnp.bfloat16)
    return pl.pallas_call(
        functools.partial(products_kernel, len(bufs), stage, first, last),
        out_shape=out,
        in_specs=[smem] * 3 + [vmem] * (len(extra) + 1) + [anywhere] * len(bufs),
        out_specs=out_specs,
        scratch_shapes=scratch,
        compiler_params=pltpu.CompilerParams(vmem_limit_bytes=16 << 20),
        cost_estimate=pl.CostEstimate(
            flops=2 * LOCAL * n_rows * WIDTH // 4,
            bytes_accessed=n_rows * WIDTH * 2 + (8 << 20),
            transcendentals=0,
        ),
    )(*scalars, *extra, tiles, *bufs)


def norm_rows(values, gain):
    scale = lax.rsqrt(jnp.mean(values * values, axis=-1, keepdims=True) + 1e-06)
    return (values * scale * gain).astype(jnp.bfloat16)


def temporal_kernel(
    rows_ref, embed_ref, gain1_ref, qkv_ref, out_w_ref, gain2_ref, up_ref, down_ref, out_ref
):
    groups = ITEMS // 8
    embed = embed_ref[...].astype(jnp.float32)
    embed = jnp.broadcast_to(embed[:, None, :], (16, 8, WIDTH)).reshape(TILE, WIDTH)
    values = rows_ref[...].astype(jnp.float32)
    mixed = jnp.concatenate(
        [values[:, g * 8 : (g + 1) * 8, :].reshape(TILE, WIDTH) + embed for g in range(groups)],
        axis=0,
    )
    normed = norm_rows(mixed, gain1_ref[...].astype(jnp.float32))
    qkv = jnp.dot(normed, qkv_ref[...], preferred_element_type=jnp.float32).astype(jnp.bfloat16)

    at = lax.broadcasted_iota(jnp.int32, (2 * TILE, TILE), 0) % TILE
    to = lax.broadcasted_iota(jnp.int32, (2 * TILE, TILE), 1)
    allowed = (at % 8 == to % 8) & (to // 8 <= at // 8)
    lane = lax.broadcasted_iota(jnp.int32, (TILE, TILE), 1)
    low_half = lane < 64
    zero = jnp.zeros((TILE, TILE), jnp.bfloat16)
    contexts = []
    for g in range(groups):
        rows = slice(g * TILE, (g + 1) * TILE)
        pieces = []
        for pair in range(4):
            query = qkv[rows, pair * TILE : (pair + 1) * TILE] * jnp.bfloat16(0.125)
            key = qkv[rows, WIDTH + pair * TILE : WIDTH + (pair + 1) * TILE]
            value = qkv[rows, 2 * WIDTH + pair * TILE : 2 * WIDTH + (pair + 1) * TILE]
            split_query = jnp.concatenate(
                [jnp.where(low_half, query, zero), jnp.where(low_half, zero, query)], axis=0
            )
            split_value = jnp.concatenate(
                [jnp.where(low_half, value, zero), jnp.where(low_half, zero, value)], axis=0
            )
            scores = lax.dot_general(
                split_query, key, (((1,), (1,)), ((), ())), preferred_element_type=jnp.float32
            )
            scores = jnp.where(allowed, scores, -1e30)
            expo = jnp.exp(scores - jnp.max(scores, axis=-1, keepdims=True))
            weights = (expo / jnp.sum(expo, axis=-1, keepdims=True)).astype(jnp.bfloat16)
            both = jnp.concatenate([weights[:TILE], weights[TILE:]], axis=1)
            pieces.append(jnp.dot(both, split_value, preferred_element_type=jnp.float32))
        contexts.append(jnp.concatenate(pieces, axis=1))
    context = jnp.concatenate(contexts, axis=0).astype(jnp.bfloat16)
    residual = mixed + jnp.dot(context, out_w_ref[...], preferred_element_type=jnp.float32)
    normed_two = norm_rows(residual, gain2_ref[...].astype(jnp.float32))
    hidden = jax.nn.gelu(
        jnp.dot(normed_two, up_ref[...], preferred_element_type=jnp.float32)
    ).astype(jnp.bfloat16)
    result = residual + jnp.dot(hidden, down_ref[...], preferred_element_type=jnp.float32)
    for g in range(groups):
        piece = result[g * TILE : (g + 1) * TILE].reshape(16, 8, WIDTH)
        out_ref[:, g * 8 : (g + 1) * 8, :] = piece.astype(jnp.bfloat16)


def temporal(rows, embed, gain1, w_qkv, w_out, gain2, w_up, w_down):
    snaps, items, width = rows.shape

    def whole(array):
        return pl.BlockSpec(array.shape, lambda i: (0,) * array.ndim, pipeline_mode=pl.Buffered(1))

    block = pl.BlockSpec((snaps, ITEMS, width), lambda i: (0, i, 0))
    weights = (embed, gain1[None, :], w_qkv, w_out, gain2[None, :], w_up, w_down)
    return pl.pallas_call(
        temporal_kernel,
        grid=(items // ITEMS,),
        out_shape=jax.ShapeDtypeStruct(rows.shape, jnp.bfloat16),
        in_specs=[block] + [whole(w) for w in weights],
        out_specs=block,
        compiler_params=pltpu.CompilerParams(vmem_limit_bytes=40 << 20),
        name="temporal",
    )(rows, *weights)


def plan(pairs, count, vertex):
    row, col = pairs[:, 0], pairs[:, 1]
    shard = col // 8
    block = col % 8
    distance = (vertex // 2 - shard // 2) % 8
    other = (shard % 2) ^ (vertex % 2)
    stage_of, place_of = [0] * 8, [0] * 8
    for s, distances in enumerate(STAGES):
        for i, d in enumerate(distances):
            stage_of[d], place_of[d] = s, i
    stage = sum(jnp.where(distance == d, stage_of[d], 0) for d in range(8))
    place = sum(jnp.where(distance == d, place_of[d], 0) for d in range(8))
    where = (place * 2 + other) * 8 + block
    index = jnp.arange(SLOTS, dtype=jnp.int32)
    n_keys = len(STAGES) * ROWS
    key = jnp.where(index < count, stage * ROWS + row, n_keys)
    code = index + (where << 7) + (1 << 13) + (row << 14)
    earlier = (key[None, :] == key[:, None]) & (index[None, :] < index[:, None])
    nth = jnp.sum(earlier.astype(jnp.int32), axis=1)
    keys = jnp.arange(n_keys, dtype=jnp.int32)
    in_key = jnp.sum((key[None, :] == keys[:, None]).astype(jnp.int32), axis=1)
    pairs_in = (in_key + 1) // 2
    ahead = (keys[None, :] // ROWS == stage[:, None]) & (keys[None, :] < key[:, None])
    base = jnp.sum(jnp.where(ahead, pairs_in[None, :], 0), axis=1)
    at = jnp.where(index < count, stage * PAIRS + base + nth // 2, -1)
    places = jnp.arange(len(STAGES) * PAIRS, dtype=jnp.int32)
    hit = places[:, None] == at[None, :]
    left = jnp.sum(jnp.where(hit & (nth % 2 == 0)[None, :], code[None, :], 0), axis=1)
    right = jnp.sum(jnp.where(hit & (nth % 2 == 1)[None, :], code[None, :], 0), axis=1)
    counts = jnp.sum(pairs_in.reshape(len(STAGES), ROWS), axis=1)
    return left, right, counts


def layer(
    features,
    tile_coord,
    tile_count,
    tile_values,
    w_agg,
    w_root,
    time_embed,
    gain_first,
    w_qkv,
    w_out,
    gain_second,
    w_up,
    w_down,
):
    own = features[0]
    tiles = tile_values[0]
    n_vertex = lax.axis_size("vertex")

    def hop(x, step):
        return lax.ppermute(x, "vertex", [(v, (v + 2 * step) % n_vertex) for v in range(n_vertex)])

    def swap(x):
        return lax.ppermute(x, "vertex", [(v, v ^ 1) for v in range(n_vertex)])

    chunks = (own[:HALF], own[HALF:])
    got = {0: (own, swap(own))}
    right, left = list(chunks), list(chunks)
    for h in (1, 2, 3):
        for c in (0, 1):
            right[c] = hop(right[c], 1)
            left[c] = hop(left[c], -1)
        got[h] = (right[0], right[1], swap(right[0]), swap(right[1]))
        got[8 - h] = (left[0], left[1], swap(left[0]), swap(left[1]))
    far = (hop(right[0], 1), hop(left[1], -1))
    got[4] = (far[0], far[1], swap(far[0]), swap(far[1]))

    scalars = plan(tile_coord[0], tile_count[0, 0], lax.axis_index("vertex"))
    bufs = [[b for d in distances for b in got[d]] for distances in STAGES]
    acc, base = products(0, scalars, (own, w_root), tiles, bufs[0], first=True)
    for s in range(1, len(STAGES) - 1):
        acc = products(s, scalars, (acc,), tiles, bufs[s])
    s = len(STAGES) - 1
    acc = products(s, scalars, (acc, base, w_agg), tiles, bufs[s], last=True)
    tm_count = lax.axis_size("tm")
    sections = acc.reshape(tm_count, LOCAL // tm_count, WIDTH)
    arrived = lax.all_to_all(sections, "tm", split_axis=0, concat_axis=0, tiled=True)
    return temporal(arrived, time_embed, gain_first, w_qkv, w_out, gain_second, w_up, w_down)


def solution(mesh):
    return jax.shard_map(
        layer,
        mesh=mesh,
        in_specs=(
            P("tm", "vertex", None),
            P("tm", "vertex", None),
            P("tm", "vertex"),
            P("tm", "vertex", None, None),
            P(),
            P(),
            P(),
            P(),
            P(),
            P(),
            P(),
            P(),
            P(),
        ),
        out_specs=P(None, ("vertex", "tm"), None),
        check_vma=False,
    )
```

```python
import functools

import jax
import jax.numpy as jnp
from jax import lax
from jax.experimental import pallas as pl
from jax.experimental.pallas import tpu as pltpu
from jax.sharding import PartitionSpec as P


TILE = 128
WIDTH = 512
LOCAL = 1024
SLOTS = 128
ROWS = LOCAL // TILE
HALF = LOCAL // 2
STAGES = (
    ((0, 0), (0, 1)),
    ((1, 0), (1, 1), (7, 0), (7, 1)),
    ((2, 0), (2, 1), (6, 0), (6, 1)),
    ((3, 0), (3, 1), (5, 0), (5, 1)),
    ((4, 0),),
    ((4, 1),),
)
PAIRS = 72
UNROLL = 4
ITEMS = 32


def in_hbm(array):
    return pltpu.with_memory_space_constraint(array, pltpu.HBM)


def products_kernel(n_bufs, stage, first, last, *refs):
    left_ref, right_ref, count_ref = refs[:3]
    refs = refs[3:]
    if first:
        root_ref, refs = refs[0], refs[1:]
    else:
        refs = refs[1:]
    if last:
        base_ref, agg_ref, refs = refs[0], refs[1], refs[2:]
    tiles, bufs, refs = refs[0], refs[1 : 1 + n_bufs], refs[1 + n_bufs :]
    if first:
        acc, base_out, *refs = refs
    elif last:
        acc, out_ref, *refs = refs
    else:
        acc, *refs = refs
    tile_buf, feat_buf, tile_sem, feat_sem = refs
    steps = (count_ref[stage] + UNROLL - 1) // UNROLL

    def tile_copy(code, place):
        return pltpu.make_async_copy(
            tiles.at[code & 127], tile_buf.at[place], tile_sem.at[place]
        )

    @pl.loop(0, steps)
    def _(step):
        for u in range(UNROLL):
            at = step * UNROLL + u
            tile_copy(left_ref[stage * PAIRS + at], 2 * at).start()
            tile_copy(right_ref[stage * PAIRS + at], 2 * at + 1).start()

    start = 0
    feature_copies = []
    for k, buf in enumerate(bufs):
        copy = pltpu.make_async_copy(
            buf, feat_buf.at[pl.ds(start, buf.shape[0])], feat_sem.at[k]
        )
        copy.start()
        feature_copies.append(copy)
        start += buf.shape[0]
    if first:
        acc[...] = jnp.zeros_like(acc)
    for copy in feature_copies:
        copy.wait()

    def half(code, place):
        tile_copy(code, place).wait()
        tile = tile_buf[place]
        live = (code >> 13) & 1
        tile = jnp.where(live == 1, tile, jnp.zeros_like(tile))
        block = pl.multiple_of(((code >> 7) & 63) * TILE, TILE)
        return tile, feat_buf[pl.ds(block, TILE), :]

    @pl.loop(0, steps)
    def _(step):
        for u in range(UNROLL):
            at = step * UNROLL + u
            code = left_ref[stage * PAIRS + at]
            tile0, feat0 = half(code, 2 * at)
            tile1, feat1 = half(right_ref[stage * PAIRS + at], 2 * at + 1)
            product = jnp.dot(
                jnp.concatenate([tile0, tile1], axis=1),
                jnp.concatenate([feat0, feat1], axis=0),
                preferred_element_type=jnp.float32,
            )
            rows = pl.ds(pl.multiple_of((code >> 14) * TILE, TILE), TILE)
            acc[rows, :] += product

    if first:

        @pl.loop(0, 4)
        def _(i):
            rows = pl.ds(pl.multiple_of(i * 256, 256), 256)
            base_out[rows, :] = jnp.dot(
                feat_buf[rows, :], root_ref[...], preferred_element_type=jnp.float32
            )

    if last:

        @pl.loop(0, 4)
        def _(i):
            rows = pl.ds(pl.multiple_of(i * 256, 256), 256)
            combined = base_ref[rows, :] + jnp.dot(
                acc[rows, :].astype(jnp.bfloat16),
                agg_ref[...],
                preferred_element_type=jnp.float32,
            )
            out_ref[rows, :] = jax.nn.gelu(combined).astype(jnp.bfloat16)


def products(stage, scalars, extra, tiles, bufs, first=False, last=False):
    n_rows = sum(b.shape[0] for b in bufs)
    smem = pl.BlockSpec(memory_space=pltpu.SMEM)
    vmem = pl.BlockSpec(memory_space=pltpu.VMEM)
    anywhere = pl.BlockSpec(memory_space=pl.ANY)
    hbm = pl.BlockSpec(memory_space=pltpu.HBM)
    scratch = [
        pltpu.VMEM((2 * PAIRS, TILE, TILE), jnp.bfloat16),
        pltpu.VMEM((n_rows, WIDTH), jnp.bfloat16),
        pltpu.SemaphoreType.DMA((2 * PAIRS,)),
        pltpu.SemaphoreType.DMA((len(bufs),)),
    ]
    partial = jax.ShapeDtypeStruct((LOCAL, WIDTH), jnp.float32)
    out, out_specs = partial, vmem
    if first:
        out, out_specs = (partial, partial), (vmem, vmem)
    if last:
        whole = jax.ShapeDtypeStruct((LOCAL, WIDTH), jnp.bfloat16)
        out, out_specs = (partial, whole), (vmem, vmem)
    return pl.pallas_call(
        functools.partial(products_kernel, len(bufs), stage, first, last),
        out_shape=out,
        in_specs=[smem] * 3 + [vmem] * len(extra) + [hbm] + [anywhere] * len(bufs),
        out_specs=out_specs,
        scratch_shapes=scratch,
        input_output_aliases={} if first else {3: 0},
        compiler_params=pltpu.CompilerParams(vmem_limit_bytes=16 << 20),
        cost_estimate=pl.CostEstimate(
            flops=2 * LOCAL * n_rows * WIDTH // 4,
            bytes_accessed=n_rows * WIDTH * 2 + (8 << 20),
            transcendentals=0,
        ),
    )(*scalars, *extra, tiles, *bufs)


def split_kernel(own, low, high, sem):
    copies = [
        pltpu.make_async_copy(own.at[pl.ds(k * HALF, HALF)], out, sem.at[k])
        for k, out in enumerate((low, high))
    ]
    for copy in copies:
        copy.start()
    for copy in copies:
        copy.wait()


def split(own):
    piece = pltpu.VMEM((HALF, WIDTH), jnp.bfloat16)
    vmem = pl.BlockSpec(memory_space=pltpu.VMEM)
    return pl.pallas_call(
        split_kernel,
        out_shape=(piece, piece),
        in_specs=[pl.BlockSpec(memory_space=pltpu.HBM)],
        out_specs=(vmem, vmem),
        scratch_shapes=[pltpu.SemaphoreType.DMA((2,))],
        compiler_params=pltpu.CompilerParams(vmem_limit_bytes=4 << 20),
        name="split",
    )(in_hbm(own))


def norm_rows(values, gain):
    scale = lax.rsqrt(jnp.mean(values * values, axis=-1, keepdims=True) + 1e-06)
    return (values * scale * gain).astype(jnp.bfloat16)


def temporal_kernel(*refs):
    rows_ref, embed_ref, gain1_ref, gain2_ref = refs[:4]
    out_ref, *buffers, sem = refs[8:]
    copies = [
        pltpu.make_async_copy(source, buffer, sem.at[k])
        for k, (source, buffer) in enumerate(zip(refs[4:8], buffers, strict=True))
    ]
    fresh = pl.program_id(0) == 0

    @pl.when(fresh)
    def _():
        for copy in copies:
            copy.start()

    def weight(k):
        pl.when(fresh)(copies[k].wait)
        return buffers[k][...]

    groups = ITEMS // 8
    embed = embed_ref[...].astype(jnp.float32)
    embed = jnp.broadcast_to(embed[:, None, :], (16, 8, WIDTH)).reshape(TILE, WIDTH)
    values = rows_ref[...].astype(jnp.float32)
    mixed = jnp.concatenate(
        [values[:, g * 8 : (g + 1) * 8, :].reshape(TILE, WIDTH) + embed for g in range(groups)],
        axis=0,
    )
    normed = norm_rows(mixed, gain1_ref[...].astype(jnp.float32))
    qkv = jnp.dot(normed, weight(0), preferred_element_type=jnp.float32).astype(jnp.bfloat16)

    at = lax.broadcasted_iota(jnp.int32, (2 * TILE, TILE), 0) % TILE
    to = lax.broadcasted_iota(jnp.int32, (2 * TILE, TILE), 1)
    allowed = (at % 8 == to % 8) & (to // 8 <= at // 8)
    lane = lax.broadcasted_iota(jnp.int32, (TILE, TILE), 1)
    low_half = lane < 64
    zero = jnp.zeros((TILE, TILE), jnp.bfloat16)
    contexts = []
    for g in range(groups):
        rows = slice(g * TILE, (g + 1) * TILE)
        pieces = []
        for pair in range(4):
            query = qkv[rows, pair * TILE : (pair + 1) * TILE] * jnp.bfloat16(0.125)
            key = qkv[rows, WIDTH + pair * TILE : WIDTH + (pair + 1) * TILE]
            value = qkv[rows, 2 * WIDTH + pair * TILE : 2 * WIDTH + (pair + 1) * TILE]
            split_query = jnp.concatenate(
                [jnp.where(low_half, query, zero), jnp.where(low_half, zero, query)], axis=0
            )
            split_value = jnp.concatenate(
                [jnp.where(low_half, value, zero), jnp.where(low_half, zero, value)], axis=0
            )
            scores = lax.dot_general(
                split_query, key, (((1,), (1,)), ((), ())), preferred_element_type=jnp.float32
            )
            scores = jnp.where(allowed, scores, -1e30)
            expo = jnp.exp(scores - jnp.max(scores, axis=-1, keepdims=True))
            weights = (expo / jnp.sum(expo, axis=-1, keepdims=True)).astype(jnp.bfloat16)
            both = jnp.concatenate([weights[:TILE], weights[TILE:]], axis=1)
            pieces.append(jnp.dot(both, split_value, preferred_element_type=jnp.float32))
        contexts.append(jnp.concatenate(pieces, axis=1))
    context = jnp.concatenate(contexts, axis=0).astype(jnp.bfloat16)
    residual = mixed + jnp.dot(context, weight(1), preferred_element_type=jnp.float32)
    normed_two = norm_rows(residual, gain2_ref[...].astype(jnp.float32))
    hidden = jax.nn.gelu(
        jnp.dot(normed_two, weight(2), preferred_element_type=jnp.float32)
    ).astype(jnp.bfloat16)
    result = residual + jnp.dot(hidden, weight(3), preferred_element_type=jnp.float32)
    for g in range(groups):
        piece = result[g * TILE : (g + 1) * TILE].reshape(16, 8, WIDTH)
        out_ref[:, g * 8 : (g + 1) * 8, :] = piece.astype(jnp.bfloat16)


def temporal(rows, weights):
    snaps, items, width = rows.shape
    hbm = pl.BlockSpec(memory_space=pltpu.HBM)
    block = pl.BlockSpec((snaps, ITEMS, width), lambda i: (0, i, 0))
    small = [pl.BlockSpec(w.shape, lambda i: (0, 0)) for w in weights[:3]]
    return pl.pallas_call(
        temporal_kernel,
        grid=(items // ITEMS,),
        out_shape=jax.ShapeDtypeStruct(rows.shape, jnp.bfloat16),
        in_specs=[block, *small] + [hbm] * 4,
        out_specs=block,
        scratch_shapes=[pltpu.VMEM(w.shape, w.dtype) for w in weights[3:]]
        + [pltpu.SemaphoreType.DMA((4,))],
        compiler_params=pltpu.CompilerParams(vmem_limit_bytes=32 << 20),
        name="temporal",
    )(rows, *weights)


def plan(pairs, count, vertex):
    row, col = pairs[:, 0], pairs[:, 1]
    shard = col // 8
    block = col % 8
    distance = (vertex // 2 - shard // 2) % 8
    other = (shard % 2) ^ (vertex % 2)
    source = distance * 2 + other
    stage_of, place_of = [0] * 16, [0] * 16
    for s, sources in enumerate(STAGES):
        for i, (d, o) in enumerate(sources):
            stage_of[d * 2 + o], place_of[d * 2 + o] = s, i
    stage = sum(jnp.where(source == k, stage_of[k], 0) for k in range(16))
    place = sum(jnp.where(source == k, place_of[k], 0) for k in range(16))
    where = place * 8 + block
    index = jnp.arange(SLOTS, dtype=jnp.int32)
    n_keys = len(STAGES) * ROWS
    key = jnp.where(index < count, stage * ROWS + row, n_keys)
    code = index + (where << 7) + (1 << 13) + (row << 14)
    earlier = (key[None, :] == key[:, None]) & (index[None, :] < index[:, None])
    nth = jnp.sum(earlier.astype(jnp.int32), axis=1)
    keys = jnp.arange(n_keys, dtype=jnp.int32)
    in_key = jnp.sum((key[None, :] == keys[:, None]).astype(jnp.int32), axis=1)
    pairs_in = (in_key + 1) // 2
    ahead = (keys[None, :] // ROWS == stage[:, None]) & (keys[None, :] < key[:, None])
    base = jnp.sum(jnp.where(ahead, pairs_in[None, :], 0), axis=1)
    at = jnp.where(index < count, stage * PAIRS + base + nth // 2, -1)
    places = jnp.arange(len(STAGES) * PAIRS, dtype=jnp.int32)
    hit = places[:, None] == at[None, :]
    left = jnp.sum(jnp.where(hit & (nth % 2 == 0)[None, :], code[None, :], 0), axis=1)
    right = jnp.sum(jnp.where(hit & (nth % 2 == 1)[None, :], code[None, :], 0), axis=1)
    counts = jnp.sum(pairs_in.reshape(len(STAGES), ROWS), axis=1)
    return left, right, counts


def layer(
    features,
    tile_coord,
    tile_count,
    tile_values,
    w_agg,
    w_root,
    time_embed,
    gain_first,
    w_qkv,
    w_out,
    gain_second,
    w_up,
    w_down,
):
    own = features[0]
    tiles = in_hbm(tile_values[0])
    n_vertex = lax.axis_size("vertex")

    def hop(x, step):
        return lax.ppermute(x, "vertex", [(v, (v + 2 * step) % n_vertex) for v in range(n_vertex)])

    def swap(x):
        return lax.ppermute(x, "vertex", [(v, v ^ 1) for v in range(n_vertex)])

    chunks = split(own)
    got = {(0, 0): (in_hbm(own),), (0, 1): (swap(own),)}
    right, left = list(chunks), list(chunks)
    for h in (1, 2, 3, 4):
        if h < 4:
            right = [hop(right[c], 1) for c in (0, 1)]
            left = [hop(left[c], -1) for c in (0, 1)]
            got[h, 0], got[8 - h, 0] = right, left
            got[h, 1] = [swap(right[c]) for c in (0, 1)]
            got[8 - h, 1] = [swap(left[c]) for c in (0, 1)]
        else:
            far = (hop(right[0], 1), hop(left[1], -1))
            got[4, 0] = far
            got[4, 1] = (swap(far[0]), swap(far[1]))

    scalars = plan(tile_coord[0], tile_count[0, 0], lax.axis_index("vertex"))
    bufs = [[b for source in sources for b in got[source]] for sources in STAGES]
    acc, base = products(0, scalars, (w_root,), tiles, bufs[0], first=True)
    for s in range(1, len(STAGES) - 1):
        acc = products(s, scalars, (acc,), tiles, bufs[s])
    s = len(STAGES) - 1
    rows = products(s, scalars, (acc, base, w_agg), tiles, bufs[s], last=True)[1]
    tm_count = lax.axis_size("tm")
    sections = rows.reshape(tm_count, LOCAL // tm_count, WIDTH)
    arrived = lax.all_to_all(sections, "tm", split_axis=0, concat_axis=0, tiled=True)
    weights = (time_embed, gain_first[None, :], gain_second[None, :])
    weights += tuple(in_hbm(w) for w in (w_qkv, w_out, w_up, w_down))
    return temporal(arrived, weights)


def solution(mesh):
    return jax.shard_map(
        layer,
        mesh=mesh,
        in_specs=(
            P("tm", "vertex", None),
            P("tm", "vertex", None),
            P("tm", "vertex"),
            P("tm", "vertex", None, None),
            P(),
            P(),
            P(),
            P(),
            P(),
            P(),
            P(),
            P(),
            P(),
        ),
        out_specs=P(None, ("vertex", "tm"), None),
        check_vma=False,
    )
```

```python
import functools

import jax
import jax.numpy as jnp
from jax import lax
from jax.experimental import pallas as pl
from jax.experimental.pallas import tpu as pltpu
from jax.sharding import PartitionSpec as P


TILE = 128
WIDTH = 512
LOCAL = 1024
SLOTS = 128
ROWS = LOCAL // TILE
HALF = LOCAL // 2
STAGES = (
    ((0, 0), (0, 1)),
    ((1, 0), (1, 1), (7, 0), (7, 1)),
    ((2, 0), (2, 1), (6, 0), (6, 1)),
    ((3, 0), (3, 1), (5, 0), (5, 1)),
    ((4, 0),),
    ((4, 1),),
)
PAIRS = 72
UNROLL = 4
ITEMS = 32


def in_hbm(array):
    return pltpu.with_memory_space_constraint(array, pltpu.HBM)


def products_kernel(n_bufs, stage, first, last, *refs):
    left_ref, right_ref, count_ref = refs[:3]
    refs = refs[3:]
    if first:
        root_ref, refs = refs[0], refs[1:]
    else:
        refs = refs[1:]
    if last:
        base_ref, agg_ref, refs = refs[0], refs[1], refs[2:]
    tiles, bufs, refs = refs[0], refs[1 : 1 + n_bufs], refs[1 + n_bufs :]
    if first:
        acc, base_out, *refs = refs
    elif last:
        acc, out_ref, *refs = refs
    else:
        acc, *refs = refs
    feat_buf, feat_sem = refs
    start = 0
    feature_copies = []
    for k, buf in enumerate(bufs):
        copy = pltpu.make_async_copy(
            buf, feat_buf.at[pl.ds(start, buf.shape[0])], feat_sem.at[k]
        )
        copy.start()
        feature_copies.append(copy)
        start += buf.shape[0]
    if first:
        acc[...] = jnp.zeros_like(acc)
    for copy in feature_copies:
        copy.wait()

    def half(code):
        tile = tiles[code & 127]
        live = (code >> 13) & 1
        tile = jnp.where(live == 1, tile, jnp.zeros_like(tile))
        block = pl.multiple_of(((code >> 7) & 63) * TILE, TILE)
        return tile, feat_buf[pl.ds(block, TILE), :]

    @pl.loop(0, (count_ref[stage] + UNROLL - 1) // UNROLL)
    def _(step):
        for u in range(UNROLL):
            at = stage * PAIRS + step * UNROLL + u
            code = left_ref[at]
            tile0, feat0 = half(code)
            tile1, feat1 = half(right_ref[at])
            product = jnp.dot(
                jnp.concatenate([tile0, tile1], axis=1),
                jnp.concatenate([feat0, feat1], axis=0),
                preferred_element_type=jnp.float32,
            )
            rows = pl.ds(pl.multiple_of((code >> 14) * TILE, TILE), TILE)
            acc[rows, :] += product

    if first:

        @pl.loop(0, 4)
        def _(i):
            rows = pl.ds(pl.multiple_of(i * 256, 256), 256)
            base_out[rows, :] = jnp.dot(
                feat_buf[rows, :], root_ref[...], preferred_element_type=jnp.float32
            )

    if last:

        @pl.loop(0, 4)
        def _(i):
            rows = pl.ds(pl.multiple_of(i * 256, 256), 256)
            combined = base_ref[rows, :] + jnp.dot(
                acc[rows, :].astype(jnp.bfloat16),
                agg_ref[...],
                preferred_element_type=jnp.float32,
            )
            out_ref[rows, :] = jax.nn.gelu(combined).astype(jnp.bfloat16)


def products(stage, scalars, extra, tiles, bufs, first=False, last=False):
    n_rows = sum(b.shape[0] for b in bufs)
    smem = pl.BlockSpec(memory_space=pltpu.SMEM)
    vmem = pl.BlockSpec(memory_space=pltpu.VMEM)
    anywhere = pl.BlockSpec(memory_space=pl.ANY)
    scratch = [
        pltpu.VMEM((n_rows, WIDTH), jnp.bfloat16),
        pltpu.SemaphoreType.DMA((len(bufs),)),
    ]
    partial = jax.ShapeDtypeStruct((LOCAL, WIDTH), jnp.float32)
    out, out_specs = partial, vmem
    if first:
        out, out_specs = (partial, partial), (vmem, vmem)
    if last:
        whole = jax.ShapeDtypeStruct((LOCAL, WIDTH), jnp.bfloat16)
        out, out_specs = (partial, whole), (vmem, vmem)
    return pl.pallas_call(
        functools.partial(products_kernel, len(bufs), stage, first, last),
        out_shape=out,
        in_specs=[smem] * 3 + [vmem] * (len(extra) + 1) + [anywhere] * len(bufs),
        out_specs=out_specs,
        scratch_shapes=scratch,
        input_output_aliases={} if first else {3: 0},
        compiler_params=pltpu.CompilerParams(vmem_limit_bytes=16 << 20),
        cost_estimate=pl.CostEstimate(
            flops=2 * LOCAL * n_rows * WIDTH // 4,
            bytes_accessed=n_rows * WIDTH * 2 + (8 << 20),
            transcendentals=0,
        ),
    )(*scalars, *extra, tiles, *bufs)


def split_kernel(own, low, high, sem):
    copies = [
        pltpu.make_async_copy(own.at[pl.ds(k * HALF, HALF)], out, sem.at[k])
        for k, out in enumerate((low, high))
    ]
    for copy in copies:
        copy.start()
    for copy in copies:
        copy.wait()


def split(own):
    piece = pltpu.VMEM((HALF, WIDTH), jnp.bfloat16)
    vmem = pl.BlockSpec(memory_space=pltpu.VMEM)
    return pl.pallas_call(
        split_kernel,
        out_shape=(piece, piece),
        in_specs=[pl.BlockSpec(memory_space=pltpu.HBM)],
        out_specs=(vmem, vmem),
        scratch_shapes=[pltpu.SemaphoreType.DMA((2,))],
        compiler_params=pltpu.CompilerParams(vmem_limit_bytes=4 << 20),
        name="split",
    )(in_hbm(own))


def norm_rows(values, gain):
    scale = lax.rsqrt(jnp.mean(values * values, axis=-1, keepdims=True) + 1e-06)
    return (values * scale * gain).astype(jnp.bfloat16)


def temporal_kernel(*refs):
    rows_ref, embed_ref, gain1_ref, gain2_ref = refs[:4]
    out_ref, *buffers, sem = refs[8:]
    copies = [
        pltpu.make_async_copy(source, buffer, sem.at[k])
        for k, (source, buffer) in enumerate(zip(refs[4:8], buffers, strict=True))
    ]
    fresh = pl.program_id(0) == 0

    @pl.when(fresh)
    def _():
        for copy in copies:
            copy.start()

    def weight(k):
        pl.when(fresh)(copies[k].wait)
        return buffers[k][...]

    groups = ITEMS // 8
    embed = embed_ref[...].astype(jnp.float32)
    embed = jnp.broadcast_to(embed[:, None, :], (16, 8, WIDTH)).reshape(TILE, WIDTH)
    values = rows_ref[...].astype(jnp.float32)
    mixed = jnp.concatenate(
        [values[:, g * 8 : (g + 1) * 8, :].reshape(TILE, WIDTH) + embed for g in range(groups)],
        axis=0,
    )
    normed = norm_rows(mixed, gain1_ref[...].astype(jnp.float32))
    qkv = jnp.dot(normed, weight(0), preferred_element_type=jnp.float32).astype(jnp.bfloat16)

    at = lax.broadcasted_iota(jnp.int32, (2 * TILE, TILE), 0) % TILE
    to = lax.broadcasted_iota(jnp.int32, (2 * TILE, TILE), 1)
    allowed = (at % 8 == to % 8) & (to // 8 <= at // 8)
    lane = lax.broadcasted_iota(jnp.int32, (TILE, TILE), 1)
    low_half = lane < 64
    zero = jnp.zeros((TILE, TILE), jnp.bfloat16)
    contexts = []
    for g in range(groups):
        rows = slice(g * TILE, (g + 1) * TILE)
        pieces = []
        for pair in range(4):
            query = qkv[rows, pair * TILE : (pair + 1) * TILE] * jnp.bfloat16(0.125)
            key = qkv[rows, WIDTH + pair * TILE : WIDTH + (pair + 1) * TILE]
            value = qkv[rows, 2 * WIDTH + pair * TILE : 2 * WIDTH + (pair + 1) * TILE]
            split_query = jnp.concatenate(
                [jnp.where(low_half, query, zero), jnp.where(low_half, zero, query)], axis=0
            )
            split_value = jnp.concatenate(
                [jnp.where(low_half, value, zero), jnp.where(low_half, zero, value)], axis=0
            )
            scores = lax.dot_general(
                split_query, key, (((1,), (1,)), ((), ())), preferred_element_type=jnp.float32
            )
            scores = jnp.where(allowed, scores, -1e30)
            expo = jnp.exp(scores - jnp.max(scores, axis=-1, keepdims=True))
            weights = (expo / jnp.sum(expo, axis=-1, keepdims=True)).astype(jnp.bfloat16)
            both = jnp.concatenate([weights[:TILE], weights[TILE:]], axis=1)
            pieces.append(jnp.dot(both, split_value, preferred_element_type=jnp.float32))
        contexts.append(jnp.concatenate(pieces, axis=1))
    context = jnp.concatenate(contexts, axis=0).astype(jnp.bfloat16)
    residual = mixed + jnp.dot(context, weight(1), preferred_element_type=jnp.float32)
    normed_two = norm_rows(residual, gain2_ref[...].astype(jnp.float32))
    hidden = jax.nn.gelu(
        jnp.dot(normed_two, weight(2), preferred_element_type=jnp.float32)
    ).astype(jnp.bfloat16)
    result = residual + jnp.dot(hidden, weight(3), preferred_element_type=jnp.float32)
    for g in range(groups):
        piece = result[g * TILE : (g + 1) * TILE].reshape(16, 8, WIDTH)
        out_ref[:, g * 8 : (g + 1) * 8, :] = piece.astype(jnp.bfloat16)


def temporal(rows, weights):
    snaps, items, width = rows.shape
    hbm = pl.BlockSpec(memory_space=pltpu.HBM)
    block = pl.BlockSpec((snaps, ITEMS, width), lambda i: (0, i, 0))
    small = [pl.BlockSpec(w.shape, lambda i: (0, 0)) for w in weights[:3]]
    return pl.pallas_call(
        temporal_kernel,
        grid=(items // ITEMS,),
        out_shape=jax.ShapeDtypeStruct(rows.shape, jnp.bfloat16),
        in_specs=[block, *small] + [hbm] * 4,
        out_specs=block,
        scratch_shapes=[pltpu.VMEM(w.shape, w.dtype) for w in weights[3:]]
        + [pltpu.SemaphoreType.DMA((4,))],
        compiler_params=pltpu.CompilerParams(vmem_limit_bytes=32 << 20),
        name="temporal",
    )(rows, *weights)


def plan(pairs, count, vertex):
    row, col = pairs[:, 0], pairs[:, 1]
    shard = col // 8
    block = col % 8
    distance = (vertex // 2 - shard // 2) % 8
    other = (shard % 2) ^ (vertex % 2)
    source = distance * 2 + other
    stage_of, place_of = [0] * 16, [0] * 16
    for s, sources in enumerate(STAGES):
        for i, (d, o) in enumerate(sources):
            stage_of[d * 2 + o], place_of[d * 2 + o] = s, i
    stage = sum(jnp.where(source == k, stage_of[k], 0) for k in range(16))
    place = sum(jnp.where(source == k, place_of[k], 0) for k in range(16))
    where = place * 8 + block
    index = jnp.arange(SLOTS, dtype=jnp.int32)
    n_keys = len(STAGES) * ROWS
    key = jnp.where(index < count, stage * ROWS + row, n_keys)
    code = index + (where << 7) + (1 << 13) + (row << 14)
    earlier = (key[None, :] == key[:, None]) & (index[None, :] < index[:, None])
    nth = jnp.sum(earlier.astype(jnp.int32), axis=1)
    keys = jnp.arange(n_keys, dtype=jnp.int32)
    in_key = jnp.sum((key[None, :] == keys[:, None]).astype(jnp.int32), axis=1)
    pairs_in = (in_key + 1) // 2
    ahead = (keys[None, :] // ROWS == stage[:, None]) & (keys[None, :] < key[:, None])
    base = jnp.sum(jnp.where(ahead, pairs_in[None, :], 0), axis=1)
    at = jnp.where(index < count, stage * PAIRS + base + nth // 2, -1)
    places = jnp.arange(len(STAGES) * PAIRS, dtype=jnp.int32)
    hit = places[:, None] == at[None, :]
    left = jnp.sum(jnp.where(hit & (nth % 2 == 0)[None, :], code[None, :], 0), axis=1)
    right = jnp.sum(jnp.where(hit & (nth % 2 == 1)[None, :], code[None, :], 0), axis=1)
    counts = jnp.sum(pairs_in.reshape(len(STAGES), ROWS), axis=1)
    return left, right, counts


def layer(
    features,
    tile_coord,
    tile_count,
    tile_values,
    w_agg,
    w_root,
    time_embed,
    gain_first,
    w_qkv,
    w_out,
    gain_second,
    w_up,
    w_down,
):
    own = features[0]
    tiles = tile_values[0]
    n_vertex = lax.axis_size("vertex")

    def hop(x, step):
        return lax.ppermute(x, "vertex", [(v, (v + 2 * step) % n_vertex) for v in range(n_vertex)])

    def swap(x):
        return lax.ppermute(x, "vertex", [(v, v ^ 1) for v in range(n_vertex)])

    chunks = split(own)
    got = {(0, 0): (in_hbm(own),), (0, 1): (swap(own),)}
    right, left = list(chunks), list(chunks)
    for h in (1, 2, 3, 4):
        if h < 4:
            right = [hop(right[c], 1) for c in (0, 1)]
            left = [hop(left[c], -1) for c in (0, 1)]
            got[h, 0], got[8 - h, 0] = right, left
            got[h, 1] = [swap(right[c]) for c in (0, 1)]
            got[8 - h, 1] = [swap(left[c]) for c in (0, 1)]
        else:
            far = (hop(right[0], 1), hop(left[1], -1))
            got[4, 0] = far
            got[4, 1] = (swap(far[0]), swap(far[1]))

    scalars = plan(tile_coord[0], tile_count[0, 0], lax.axis_index("vertex"))
    bufs = [[b for source in sources for b in got[source]] for sources in STAGES]
    acc, base = products(0, scalars, (w_root,), tiles, bufs[0], first=True)
    for s in range(1, len(STAGES) - 1):
        acc = products(s, scalars, (acc,), tiles, bufs[s])
    s = len(STAGES) - 1
    rows = products(s, scalars, (acc, base, w_agg), tiles, bufs[s], last=True)[1]
    tm_count = lax.axis_size("tm")
    sections = rows.reshape(tm_count, LOCAL // tm_count, WIDTH)
    arrived = lax.all_to_all(sections, "tm", split_axis=0, concat_axis=0, tiled=True)
    weights = (time_embed, gain_first[None, :], gain_second[None, :])
    weights += tuple(in_hbm(w) for w in (w_qkv, w_out, w_up, w_down))
    return temporal(arrived, weights)


def solution(mesh):
    return jax.shard_map(
        layer,
        mesh=mesh,
        in_specs=(
            P("tm", "vertex", None),
            P("tm", "vertex", None),
            P("tm", "vertex"),
            P("tm", "vertex", None, None),
            P(),
            P(),
            P(),
            P(),
            P(),
            P(),
            P(),
            P(),
            P(),
        ),
        out_specs=P(None, ("vertex", "tm"), None),
        check_vma=False,
    )
```

```python
import functools

import jax
import jax.numpy as jnp
from jax import lax
from jax.experimental import pallas as pl
from jax.experimental.pallas import tpu as pltpu
from jax.sharding import PartitionSpec as P


TILE = 128
WIDTH = 512
LOCAL = 1024
SLOTS = 128
ROWS = LOCAL // TILE
HALF = LOCAL // 2
STAGES = (
    ((0, 0), (0, 1)),
    ((1, 0), (1, 1), (7, 0), (7, 1)),
    ((2, 0), (2, 1), (6, 0), (6, 1)),
    ((3, 0), (3, 1), (5, 0), (5, 1)),
    ((4, 0),),
    ((4, 1),),
)
PAIRS = 72
UNROLL = 4
FFN_PARTS = 4


def in_hbm(array):
    return pltpu.with_memory_space_constraint(array, pltpu.HBM)


def products_kernel(n_bufs, stage, first, last, *refs):
    left_ref, right_ref, count_ref = refs[:3]
    refs = refs[3:]
    if first:
        root_ref, refs = refs[0], refs[1:]
    else:
        refs = refs[1:]
    if last:
        base_ref, agg_ref, refs = refs[0], refs[1], refs[2:]
    tiles, bufs, refs = refs[0], refs[1 : 1 + n_bufs], refs[1 + n_bufs :]
    if first:
        acc, base_out, *refs = refs
    elif last:
        acc, out_ref, *refs, out_buf, out_sem = refs
    else:
        acc, *refs = refs
    feat_buf, feat_sem = refs
    start = 0
    feature_copies = []
    for k, buf in enumerate(bufs):
        copy = pltpu.make_async_copy(
            buf, feat_buf.at[pl.ds(start, buf.shape[0])], feat_sem.at[k]
        )
        copy.start()
        feature_copies.append(copy)
        start += buf.shape[0]
    if first:
        acc[...] = jnp.zeros_like(acc)
    for copy in feature_copies:
        copy.wait()

    def half(code):
        tile = tiles[code & 127]
        live = (code >> 13) & 1
        tile = jnp.where(live == 1, tile, jnp.zeros_like(tile))
        block = pl.multiple_of(((code >> 7) & 63) * TILE, TILE)
        return tile, feat_buf[pl.ds(block, TILE), :]

    @pl.loop(0, (count_ref[stage] + UNROLL - 1) // UNROLL)
    def _(step):
        for u in range(UNROLL):
            at = stage * PAIRS + step * UNROLL + u
            code = left_ref[at]
            tile0, feat0 = half(code)
            tile1, feat1 = half(right_ref[at])
            product = jnp.dot(
                jnp.concatenate([tile0, tile1], axis=1),
                jnp.concatenate([feat0, feat1], axis=0),
                preferred_element_type=jnp.float32,
            )
            rows = pl.ds(pl.multiple_of((code >> 14) * TILE, TILE), TILE)
            acc[rows, :] += product

    if first:

        @pl.loop(0, 4)
        def _(i):
            rows = pl.ds(pl.multiple_of(i * 256, 256), 256)
            base_out[rows, :] = jnp.dot(
                feat_buf[rows, :], root_ref[...], preferred_element_type=jnp.float32
            )

    if last:
        out_copies = []
        for i in range(4):
            rows = slice(i * 256, (i + 1) * 256)
            combined = base_ref[rows, :] + jnp.dot(
                acc[rows, :].astype(jnp.bfloat16),
                agg_ref[...],
                preferred_element_type=jnp.float32,
            )
            out_buf[rows, :] = jax.nn.gelu(combined).astype(jnp.bfloat16)
            span = pl.ds(i * 256, 256)
            copy = pltpu.make_async_copy(out_buf.at[span], out_ref.at[span], out_sem.at[i])
            copy.start()
            out_copies.append(copy)
        for copy in out_copies:
            copy.wait()


def products(stage, scalars, extra, tiles, bufs, first=False, last=False):
    n_rows = sum(b.shape[0] for b in bufs)
    smem = pl.BlockSpec(memory_space=pltpu.SMEM)
    vmem = pl.BlockSpec(memory_space=pltpu.VMEM)
    anywhere = pl.BlockSpec(memory_space=pl.ANY)
    scratch = [
        pltpu.VMEM((n_rows, WIDTH), jnp.bfloat16),
        pltpu.SemaphoreType.DMA((len(bufs),)),
    ]
    partial = jax.ShapeDtypeStruct((LOCAL, WIDTH), jnp.float32)
    out, out_specs = partial, vmem
    if first:
        out, out_specs = (partial, partial), (vmem, vmem)
    if last:
        whole = pltpu.HBM((LOCAL, WIDTH), jnp.bfloat16)
        out, out_specs = (partial, whole), (vmem, pl.BlockSpec(memory_space=pltpu.HBM))
        scratch += [
            pltpu.VMEM((LOCAL, WIDTH), jnp.bfloat16),
            pltpu.SemaphoreType.DMA((4,)),
        ]
    return pl.pallas_call(
        functools.partial(products_kernel, len(bufs), stage, first, last),
        out_shape=out,
        in_specs=[smem] * 3 + [vmem] * (len(extra) + 1) + [anywhere] * len(bufs),
        out_specs=out_specs,
        scratch_shapes=scratch,
        input_output_aliases={} if first else {3: 0},
        compiler_params=pltpu.CompilerParams(vmem_limit_bytes=16 << 20),
        cost_estimate=pl.CostEstimate(
            flops=2 * LOCAL * n_rows * WIDTH // 4,
            bytes_accessed=n_rows * WIDTH * 2 + (8 << 20),
            transcendentals=0,
        ),
    )(*scalars, *extra, tiles, *bufs)


def split_kernel(own, low, high, sem):
    copies = [
        pltpu.make_async_copy(own.at[pl.ds(k * HALF, HALF)], out, sem.at[k])
        for k, out in enumerate((low, high))
    ]
    for copy in copies:
        copy.start()
    for copy in copies:
        copy.wait()


def split(own):
    piece = pltpu.VMEM((HALF, WIDTH), jnp.bfloat16)
    vmem = pl.BlockSpec(memory_space=pltpu.VMEM)
    return pl.pallas_call(
        split_kernel,
        out_shape=(piece, piece),
        in_specs=[pl.BlockSpec(memory_space=pltpu.HBM)],
        out_specs=(vmem, vmem),
        scratch_shapes=[pltpu.SemaphoreType.DMA((2,))],
        compiler_params=pltpu.CompilerParams(vmem_limit_bytes=4 << 20),
        name="split",
    )(in_hbm(own))


def norm_rows(values, gain):
    scale = lax.rsqrt(jnp.mean(values * values, axis=-1, keepdims=True) + 1e-06)
    return (values * scale * gain).astype(jnp.bfloat16)


def temporal_kernel(
    rows_ref, embed_ref, gain1_ref, gain2_ref, qkv_ref, out_w_ref, up_hbm, down_hbm, out_ref, *scratch
):
    up_ref, down_ref, out_buf, weight_sem, out_sem = scratch
    late = [
        pltpu.make_async_copy(source, target, weight_sem.at[k])
        for k, (source, target) in enumerate(((up_hbm, up_ref), (down_hbm, down_ref)))
    ]
    for copy in late:
        copy.start()
    items = rows_ref.shape[1]
    groups = items // 8
    embed = embed_ref[...].astype(jnp.float32)
    embed = jnp.broadcast_to(embed[:, None, :], (16, 8, WIDTH)).reshape(TILE, WIDTH)
    values = rows_ref[...].astype(jnp.float32)
    mixed = jnp.concatenate(
        [values[:, g * 8 : (g + 1) * 8, :].reshape(TILE, WIDTH) + embed for g in range(groups)],
        axis=0,
    )
    normed = norm_rows(mixed, gain1_ref[...].astype(jnp.float32))
    qkv = jnp.dot(normed, qkv_ref[...], preferred_element_type=jnp.float32).astype(jnp.bfloat16)

    at = lax.broadcasted_iota(jnp.int32, (2 * TILE, TILE), 0) % TILE
    to = lax.broadcasted_iota(jnp.int32, (2 * TILE, TILE), 1)
    allowed = (at % 8 == to % 8) & (to // 8 <= at // 8)
    lane = lax.broadcasted_iota(jnp.int32, (TILE, TILE), 1)
    low_half = lane < 64
    zero = jnp.zeros((TILE, TILE), jnp.bfloat16)
    contexts = []
    for g in range(groups):
        rows = slice(g * TILE, (g + 1) * TILE)
        pieces = []
        for pair in range(4):
            query = qkv[rows, pair * TILE : (pair + 1) * TILE] * jnp.bfloat16(0.125)
            key = qkv[rows, WIDTH + pair * TILE : WIDTH + (pair + 1) * TILE]
            value = qkv[rows, 2 * WIDTH + pair * TILE : 2 * WIDTH + (pair + 1) * TILE]
            split_query = jnp.concatenate(
                [jnp.where(low_half, query, zero), jnp.where(low_half, zero, query)], axis=0
            )
            split_value = jnp.concatenate(
                [jnp.where(low_half, value, zero), jnp.where(low_half, zero, value)], axis=0
            )
            scores = lax.dot_general(
                split_query, key, (((1,), (1,)), ((), ())), preferred_element_type=jnp.float32
            )
            scores = jnp.where(allowed, scores, -1e30)
            expo = jnp.exp(scores - jnp.max(scores, axis=-1, keepdims=True))
            weights = (expo / jnp.sum(expo, axis=-1, keepdims=True)).astype(jnp.bfloat16)
            both = jnp.concatenate([weights[:TILE], weights[TILE:]], axis=1)
            pieces.append(jnp.dot(both, split_value, preferred_element_type=jnp.float32))
        contexts.append(jnp.concatenate(pieces, axis=1))
    context = jnp.concatenate(contexts, axis=0).astype(jnp.bfloat16)
    residual = mixed + jnp.dot(context, out_w_ref[...], preferred_element_type=jnp.float32)
    normed_two = norm_rows(residual, gain2_ref[...].astype(jnp.float32))
    for copy in late:
        copy.wait()
    count = groups // FFN_PARTS
    out_copies = []
    for part in range(FFN_PARTS):
        rows = slice(part * count * TILE, (part + 1) * count * TILE)
        hidden = jax.nn.gelu(
            jnp.dot(normed_two[rows], up_ref[...], preferred_element_type=jnp.float32)
        ).astype(jnp.bfloat16)
        result = residual[rows] + jnp.dot(
            hidden, down_ref[...], preferred_element_type=jnp.float32
        )
        for k in range(count):
            g = part * count + k
            piece = result[k * TILE : (k + 1) * TILE].reshape(16, 8, WIDTH)
            out_buf[:, g * 8 : (g + 1) * 8, :] = piece.astype(jnp.bfloat16)
        span = pl.ds(part * count * 8, count * 8)
        copy = pltpu.make_async_copy(
            out_buf.at[:, span, :], out_ref.at[:, span, :], out_sem.at[part]
        )
        copy.start()
        out_copies.append(copy)
    for copy in out_copies:
        copy.wait()


def temporal(rows, weights):
    hbm = pl.BlockSpec(memory_space=pltpu.HBM)
    vmem = pl.BlockSpec(memory_space=pltpu.VMEM)
    up, down = (in_hbm(w) for w in weights[-2:])
    return pl.pallas_call(
        temporal_kernel,
        out_shape=jax.ShapeDtypeStruct(rows.shape, jnp.bfloat16),
        in_specs=[vmem] * 6 + [hbm] * 2,
        out_specs=hbm,
        scratch_shapes=[
            pltpu.VMEM(up.shape, up.dtype),
            pltpu.VMEM(down.shape, down.dtype),
            pltpu.VMEM(rows.shape, rows.dtype),
            pltpu.SemaphoreType.DMA((2,)),
            pltpu.SemaphoreType.DMA((FFN_PARTS,)),
        ],
        compiler_params=pltpu.CompilerParams(vmem_limit_bytes=32 << 20),
        name="temporal",
    )(rows, *weights[:-2], up, down)


def plan(pairs, count, vertex):
    row, col = pairs[:, 0], pairs[:, 1]
    shard = col // 8
    block = col % 8
    distance = (vertex // 2 - shard // 2) % 8
    other = (shard % 2) ^ (vertex % 2)
    source = distance * 2 + other
    stage_of, place_of = [0] * 16, [0] * 16
    for s, sources in enumerate(STAGES):
        for i, (d, o) in enumerate(sources):
            stage_of[d * 2 + o], place_of[d * 2 + o] = s, i
    stage = sum(jnp.where(source == k, stage_of[k], 0) for k in range(16))
    place = sum(jnp.where(source == k, place_of[k], 0) for k in range(16))
    where = place * 8 + block
    index = jnp.arange(SLOTS, dtype=jnp.int32)
    n_keys = len(STAGES) * ROWS
    key = jnp.where(index < count, stage * ROWS + row, n_keys)
    code = index + (where << 7) + (1 << 13) + (row << 14)
    earlier = (key[None, :] == key[:, None]) & (index[None, :] < index[:, None])
    nth = jnp.sum(earlier.astype(jnp.int32), axis=1)
    keys = jnp.arange(n_keys, dtype=jnp.int32)
    in_key = jnp.sum((key[None, :] == keys[:, None]).astype(jnp.int32), axis=1)
    pairs_in = (in_key + 1) // 2
    ahead = (keys[None, :] // ROWS == stage[:, None]) & (keys[None, :] < key[:, None])
    base = jnp.sum(jnp.where(ahead, pairs_in[None, :], 0), axis=1)
    at = jnp.where(index < count, stage * PAIRS + base + nth // 2, -1)
    places = jnp.arange(len(STAGES) * PAIRS, dtype=jnp.int32)
    hit = places[:, None] == at[None, :]
    left = jnp.sum(jnp.where(hit & (nth % 2 == 0)[None, :], code[None, :], 0), axis=1)
    right = jnp.sum(jnp.where(hit & (nth % 2 == 1)[None, :], code[None, :], 0), axis=1)
    counts = jnp.sum(pairs_in.reshape(len(STAGES), ROWS), axis=1)
    return left, right, counts


def layer(
    features,
    tile_coord,
    tile_count,
    tile_values,
    w_agg,
    w_root,
    time_embed,
    gain_first,
    w_qkv,
    w_out,
    gain_second,
    w_up,
    w_down,
):
    own = features[0]
    tiles = tile_values[0]
    n_vertex = lax.axis_size("vertex")

    def hop(x, step):
        return lax.ppermute(x, "vertex", [(v, (v + 2 * step) % n_vertex) for v in range(n_vertex)])

    def swap(x):
        return lax.ppermute(x, "vertex", [(v, v ^ 1) for v in range(n_vertex)])

    chunks = split(own)
    got = {(0, 0): (in_hbm(own),), (0, 1): (swap(own),)}
    right, left = list(chunks), list(chunks)
    for h in (1, 2, 3, 4):
        if h < 4:
            right = [hop(right[c], 1) for c in (0, 1)]
            left = [hop(left[c], -1) for c in (0, 1)]
            got[h, 0], got[8 - h, 0] = right, left
            got[h, 1] = [swap(right[c]) for c in (0, 1)]
            got[8 - h, 1] = [swap(left[c]) for c in (0, 1)]
        else:
            far = (hop(right[0], 1), hop(left[1], -1))
            got[4, 0] = far
            got[4, 1] = (swap(far[0]), swap(far[1]))

    scalars = plan(tile_coord[0], tile_count[0, 0], lax.axis_index("vertex"))
    bufs = [[b for source in sources for b in got[source]] for sources in STAGES]
    acc, base = products(0, scalars, (w_root,), tiles, bufs[0], first=True)
    for s in range(1, len(STAGES) - 1):
        acc = products(s, scalars, (acc,), tiles, bufs[s])
    s = len(STAGES) - 1
    rows = products(s, scalars, (acc, base, w_agg), tiles, bufs[s], last=True)[1]
    tm_count = lax.axis_size("tm")
    sections = rows.reshape(tm_count, LOCAL // tm_count, WIDTH)
    arrived = lax.all_to_all(sections, "tm", split_axis=0, concat_axis=0, tiled=True)
    weights = (time_embed, gain_first[None, :], gain_second[None, :])
    weights += (w_qkv, w_out, w_up, w_down)
    return temporal(arrived, weights)


def solution(mesh):
    return jax.shard_map(
        layer,
        mesh=mesh,
        in_specs=(
            P("tm", "vertex", None),
            P("tm", "vertex", None),
            P("tm", "vertex"),
            P("tm", "vertex", None, None),
            P(),
            P(),
            P(),
            P(),
            P(),
            P(),
            P(),
            P(),
            P(),
        ),
        out_specs=P(None, ("vertex", "tm"), None),
        check_vma=False,
    )
```

```python
import functools

import jax
import jax.numpy as jnp
from jax import lax
from jax.experimental import pallas as pl
from jax.experimental.pallas import tpu as pltpu
from jax.sharding import PartitionSpec as P


TILE = 128
WIDTH = 512
LOCAL = 1024
SLOTS = 128
ROWS = LOCAL // TILE
HALF = LOCAL // 2
STAGES = (
    ((0, 0), (0, 1)),
    ((1, 0), (1, 1), (7, 0), (7, 1)),
    ((2, 0), (2, 1), (6, 0), (6, 1)),
    ((3, 0), (3, 1), (5, 0), (5, 1)),
    ((4, 0),),
    ((4, 1),),
)
PAIRS = 72
UNROLL = 4
CODES = 2 * len(STAGES) * PAIRS
FFN_PARTS = 4


def in_hbm(array):
    return pltpu.with_memory_space_constraint(array, pltpu.HBM)


def products_kernel(n_bufs, stage, first, last, *refs):
    code_ref, refs = refs[0], refs[1:]
    if first:
        root_ref, refs = refs[0], refs[1:]
    else:
        refs = refs[1:]
    if last:
        base_ref, agg_ref, refs = refs[0], refs[1], refs[2:]
    tiles, bufs, refs = refs[0], refs[1 : 1 + n_bufs], refs[1 + n_bufs :]
    if first:
        acc, base_out, *refs = refs
    elif last:
        acc, out_ref, *refs, out_buf, out_sem = refs
    else:
        acc, *refs = refs
    feat_buf, feat_sem = refs
    start = 0
    feature_copies = []
    for k, buf in enumerate(bufs):
        copy = pltpu.make_async_copy(
            buf, feat_buf.at[pl.ds(start, buf.shape[0])], feat_sem.at[k]
        )
        copy.start()
        feature_copies.append(copy)
        start += buf.shape[0]
    if first:
        acc[...] = jnp.zeros_like(acc)
    for copy in feature_copies:
        copy.wait()

    def half(code):
        tile = tiles[code & 127]
        live = (code >> 13) & 1
        tile = jnp.where(live == 1, tile, jnp.zeros_like(tile))
        block = pl.multiple_of(((code >> 7) & 63) * TILE, TILE)
        return tile, feat_buf[pl.ds(block, TILE), :]

    @pl.loop(0, (code_ref[CODES + stage] + UNROLL - 1) // UNROLL)
    def _(step):
        for u in range(UNROLL):
            at = 2 * (stage * PAIRS + step * UNROLL + u)
            code = code_ref[at]
            tile0, feat0 = half(code)
            tile1, feat1 = half(code_ref[at + 1])
            product = jnp.dot(
                jnp.concatenate([tile0, tile1], axis=1),
                jnp.concatenate([feat0, feat1], axis=0),
                preferred_element_type=jnp.float32,
            )
            rows = pl.ds(pl.multiple_of((code >> 14) * TILE, TILE), TILE)
            acc[rows, :] += product

    if first:

        @pl.loop(0, 4)
        def _(i):
            rows = pl.ds(pl.multiple_of(i * 256, 256), 256)
            base_out[rows, :] = jnp.dot(
                feat_buf[rows, :], root_ref[...], preferred_element_type=jnp.float32
            )

    if last:
        out_copies = []
        for i in range(4):
            rows = slice(i * 256, (i + 1) * 256)
            combined = base_ref[rows, :] + jnp.dot(
                acc[rows, :].astype(jnp.bfloat16),
                agg_ref[...],
                preferred_element_type=jnp.float32,
            )
            out_buf[rows, :] = jax.nn.gelu(combined).astype(jnp.bfloat16)
            span = pl.ds(i * 256, 256)
            copy = pltpu.make_async_copy(out_buf.at[span], out_ref.at[span], out_sem.at[i])
            copy.start()
            out_copies.append(copy)
        for copy in out_copies:
            copy.wait()


def products(stage, codes, extra, tiles, bufs, first=False, last=False):
    n_rows = sum(b.shape[0] for b in bufs)
    smem = pl.BlockSpec(memory_space=pltpu.SMEM)
    vmem = pl.BlockSpec(memory_space=pltpu.VMEM)
    anywhere = pl.BlockSpec(memory_space=pl.ANY)
    scratch = [
        pltpu.VMEM((n_rows, WIDTH), jnp.bfloat16),
        pltpu.SemaphoreType.DMA((len(bufs),)),
    ]
    partial = jax.ShapeDtypeStruct((LOCAL, WIDTH), jnp.float32)
    out, out_specs = partial, vmem
    if first:
        out, out_specs = (partial, partial), (vmem, vmem)
    if last:
        whole = pltpu.HBM((LOCAL, WIDTH), jnp.bfloat16)
        out, out_specs = (partial, whole), (vmem, pl.BlockSpec(memory_space=pltpu.HBM))
        scratch += [
            pltpu.VMEM((LOCAL, WIDTH), jnp.bfloat16),
            pltpu.SemaphoreType.DMA((4,)),
        ]
    return pl.pallas_call(
        functools.partial(products_kernel, len(bufs), stage, first, last),
        out_shape=out,
        in_specs=[smem] + [vmem] * (len(extra) + 1) + [anywhere] * len(bufs),
        out_specs=out_specs,
        scratch_shapes=scratch,
        input_output_aliases={} if first else {1: 0},
        compiler_params=pltpu.CompilerParams(vmem_limit_bytes=16 << 20),
        cost_estimate=pl.CostEstimate(
            flops=2 * LOCAL * n_rows * WIDTH // 4,
            bytes_accessed=n_rows * WIDTH * 2 + (8 << 20),
            transcendentals=0,
        ),
    )(codes, *extra, tiles, *bufs)


def split_kernel(own, low, high, sem):
    copies = [
        pltpu.make_async_copy(own.at[pl.ds(k * HALF, HALF)], out, sem.at[k])
        for k, out in enumerate((low, high))
    ]
    for copy in copies:
        copy.start()
    for copy in copies:
        copy.wait()


def split(own):
    piece = pltpu.VMEM((HALF, WIDTH), jnp.bfloat16)
    vmem = pl.BlockSpec(memory_space=pltpu.VMEM)
    return pl.pallas_call(
        split_kernel,
        out_shape=(piece, piece),
        in_specs=[pl.BlockSpec(memory_space=pltpu.HBM)],
        out_specs=(vmem, vmem),
        scratch_shapes=[pltpu.SemaphoreType.DMA((2,))],
        compiler_params=pltpu.CompilerParams(vmem_limit_bytes=4 << 20),
        name="split",
    )(in_hbm(own))


def norm_rows(values, gain):
    scale = lax.rsqrt(jnp.mean(values * values, axis=-1, keepdims=True) + 1e-06)
    return (values * scale * gain).astype(jnp.bfloat16)


def temporal_kernel(
    rows_ref, embed_ref, gain1_ref, gain2_ref, qkv_ref, out_w_ref, up_hbm, down_hbm, out_ref, *scratch
):
    up_ref, down_ref, out_buf, weight_sem, out_sem = scratch
    late = [
        pltpu.make_async_copy(source, target, weight_sem.at[k])
        for k, (source, target) in enumerate(((up_hbm, up_ref), (down_hbm, down_ref)))
    ]
    for copy in late:
        copy.start()
    items = rows_ref.shape[1]
    groups = items // 8
    embed = embed_ref[...].astype(jnp.float32)
    embed = jnp.broadcast_to(embed[:, None, :], (16, 8, WIDTH)).reshape(TILE, WIDTH)
    values = rows_ref[...].astype(jnp.float32)
    mixed = jnp.concatenate(
        [values[:, g * 8 : (g + 1) * 8, :].reshape(TILE, WIDTH) + embed for g in range(groups)],
        axis=0,
    )
    normed = norm_rows(mixed, gain1_ref[...].astype(jnp.float32))
    qkv = jnp.dot(normed, qkv_ref[...], preferred_element_type=jnp.float32).astype(jnp.bfloat16)

    at = lax.broadcasted_iota(jnp.int32, (2 * TILE, TILE), 0) % TILE
    to = lax.broadcasted_iota(jnp.int32, (2 * TILE, TILE), 1)
    allowed = (at % 8 == to % 8) & (to // 8 <= at // 8)
    lane = lax.broadcasted_iota(jnp.int32, (TILE, TILE), 1)
    low_half = lane < 64
    zero = jnp.zeros((TILE, TILE), jnp.bfloat16)
    contexts = []
    for g in range(groups):
        if g == groups // 2:
            for copy in late:
                copy.wait()
        rows = slice(g * TILE, (g + 1) * TILE)
        pieces = []
        for pair in range(4):
            query = qkv[rows, pair * TILE : (pair + 1) * TILE] * jnp.bfloat16(0.125)
            key = qkv[rows, WIDTH + pair * TILE : WIDTH + (pair + 1) * TILE]
            value = qkv[rows, 2 * WIDTH + pair * TILE : 2 * WIDTH + (pair + 1) * TILE]
            split_query = jnp.concatenate(
                [jnp.where(low_half, query, zero), jnp.where(low_half, zero, query)], axis=0
            )
            split_value = jnp.concatenate(
                [jnp.where(low_half, value, zero), jnp.where(low_half, zero, value)], axis=0
            )
            scores = lax.dot_general(
                split_query, key, (((1,), (1,)), ((), ())), preferred_element_type=jnp.float32
            )
            scores = jnp.where(allowed, scores, -1e30)
            expo = jnp.exp(scores - jnp.max(scores, axis=-1, keepdims=True))
            weights = (expo / jnp.sum(expo, axis=-1, keepdims=True)).astype(jnp.bfloat16)
            both = jnp.concatenate([weights[:TILE], weights[TILE:]], axis=1)
            pieces.append(jnp.dot(both, split_value, preferred_element_type=jnp.float32))
        contexts.append(jnp.concatenate(pieces, axis=1))
    context = jnp.concatenate(contexts, axis=0).astype(jnp.bfloat16)
    residual = mixed + jnp.dot(context, out_w_ref[...], preferred_element_type=jnp.float32)
    normed_two = norm_rows(residual, gain2_ref[...].astype(jnp.float32))
    count = groups // FFN_PARTS
    out_copies = []
    for part in range(FFN_PARTS):
        rows = slice(part * count * TILE, (part + 1) * count * TILE)
        hidden = jax.nn.gelu(
            jnp.dot(normed_two[rows], up_ref[...], preferred_element_type=jnp.float32)
        ).astype(jnp.bfloat16)
        result = residual[rows] + jnp.dot(
            hidden, down_ref[...], preferred_element_type=jnp.float32
        )
        for k in range(count):
            g = part * count + k
            piece = result[k * TILE : (k + 1) * TILE].reshape(16, 8, WIDTH)
            out_buf[:, g * 8 : (g + 1) * 8, :] = piece.astype(jnp.bfloat16)
        span = pl.ds(part * count * 8, count * 8)
        copy = pltpu.make_async_copy(
            out_buf.at[:, span, :], out_ref.at[:, span, :], out_sem.at[part]
        )
        copy.start()
        out_copies.append(copy)
    for copy in out_copies:
        copy.wait()


def temporal(rows, weights):
    hbm = pl.BlockSpec(memory_space=pltpu.HBM)
    vmem = pl.BlockSpec(memory_space=pltpu.VMEM)
    up, down = (in_hbm(w) for w in weights[-2:])
    return pl.pallas_call(
        temporal_kernel,
        out_shape=jax.ShapeDtypeStruct(rows.shape, jnp.bfloat16),
        in_specs=[vmem] * 6 + [hbm] * 2,
        out_specs=hbm,
        scratch_shapes=[
            pltpu.VMEM(up.shape, up.dtype),
            pltpu.VMEM(down.shape, down.dtype),
            pltpu.VMEM(rows.shape, rows.dtype),
            pltpu.SemaphoreType.DMA((2,)),
            pltpu.SemaphoreType.DMA((FFN_PARTS,)),
        ],
        compiler_params=pltpu.CompilerParams(vmem_limit_bytes=32 << 20),
        name="temporal",
    )(rows, *weights[:-2], up, down)


def plan_kernel(coord_ref, count_ref, out_ref, key_ref, size_ref, next_ref):
    vertex = lax.axis_index("vertex")
    count = count_ref[0, 0]
    n_keys = len(STAGES) * ROWS
    for k in range(n_keys + 1):
        size_ref[k] = 0

    @pl.loop(0, SLOTS, unroll=8)
    def _(slot):
        row, col = coord_ref[0, slot], coord_ref[1, slot]
        distance = ((vertex >> 1) - (col >> 4)) & 7
        other = ((col >> 3) ^ vertex) & 1
        near = jnp.minimum(distance, 8 - distance)
        far = distance == 4
        stage = near + jnp.where(far, other, 0)
        place = jnp.where(far, 0, jnp.where(distance > 4, 2, 0) + other)
        key = jnp.where(slot < count, stage * ROWS + row, n_keys)
        key_ref[slot] = key
        next_ref[slot] = slot + ((place * 8 + (col & 7)) << 7) + (1 << 13) + (row << 14)
        size_ref[key] = size_ref[key] + 1

    for stage in range(len(STAGES)):
        at = stage * PAIRS
        for key in range(stage * ROWS, (stage + 1) * ROWS):
            size = size_ref[key]
            size_ref[key] = 2 * at
            at = at + ((size + 1) >> 1)
            last = jnp.maximum(at - 1, 0)

            @pl.when((size & 1) == 1)
            def _(last=last):
                out_ref[2 * last + 1] = 0

        out_ref[CODES + stage] = at - stage * PAIRS
        for pad in range(UNROLL - 1):
            out_ref[2 * (at + pad)] = 0
            out_ref[2 * (at + pad) + 1] = 0
    size_ref[n_keys] = CODES + 8

    @pl.loop(0, SLOTS, unroll=8)
    def _(slot):
        key = key_ref[slot]
        at = size_ref[key]
        size_ref[key] = at + 1
        out_ref[at] = next_ref[slot]


def plan(pairs, count):
    smem = pl.BlockSpec(memory_space=pltpu.SMEM)
    return pl.pallas_call(
        plan_kernel,
        out_shape=jax.ShapeDtypeStruct((CODES + 8 + SLOTS,), jnp.int32),
        in_specs=[smem, smem],
        out_specs=smem,
        scratch_shapes=[pltpu.SMEM((SLOTS,), jnp.int32)] * 3,
        compiler_params=pltpu.CompilerParams(vmem_limit_bytes=1 << 20),
        cost_estimate=pl.CostEstimate(flops=1 << 20, bytes_accessed=1 << 20, transcendentals=0),
        name="plan",
    )(pairs.T, count)


def layer(
    features,
    tile_coord,
    tile_count,
    tile_values,
    w_agg,
    w_root,
    time_embed,
    gain_first,
    w_qkv,
    w_out,
    gain_second,
    w_up,
    w_down,
):
    own = features[0]
    tiles = tile_values[0]
    n_vertex = lax.axis_size("vertex")

    def hop(x, step):
        return lax.ppermute(x, "vertex", [(v, (v + 2 * step) % n_vertex) for v in range(n_vertex)])

    def swap(x):
        return lax.ppermute(x, "vertex", [(v, v ^ 1) for v in range(n_vertex)])

    chunks = split(own)
    got = {(0, 0): (in_hbm(own),), (0, 1): (swap(own),)}
    right, left = list(chunks), list(chunks)
    for h in (1, 2, 3, 4):
        if h < 4:
            right = [hop(right[c], 1) for c in (0, 1)]
            left = [hop(left[c], -1) for c in (0, 1)]
            got[h, 0], got[8 - h, 0] = right, left
            got[h, 1] = [swap(right[c]) for c in (0, 1)]
            got[8 - h, 1] = [swap(left[c]) for c in (0, 1)]
        else:
            far = (hop(right[0], 1), hop(left[1], -1))
            got[4, 0] = far
            got[4, 1] = (swap(far[0]), swap(far[1]))

    codes = plan(tile_coord[0], tile_count)
    bufs = [[b for source in sources for b in got[source]] for sources in STAGES]
    acc, base = products(0, codes, (w_root,), tiles, bufs[0], first=True)
    for s in range(1, len(STAGES) - 1):
        acc = products(s, codes, (acc,), tiles, bufs[s])
    s = len(STAGES) - 1
    rows = products(s, codes, (acc, base, w_agg), tiles, bufs[s], last=True)[1]
    tm_count = lax.axis_size("tm")
    sections = rows.reshape(tm_count, LOCAL // tm_count, WIDTH)
    arrived = lax.all_to_all(sections, "tm", split_axis=0, concat_axis=0, tiled=True)
    weights = (time_embed, gain_first[None, :], gain_second[None, :])
    weights += (w_qkv, w_out, w_up, w_down)
    return temporal(arrived, weights)


def solution(mesh):
    return jax.shard_map(
        layer,
        mesh=mesh,
        in_specs=(
            P("tm", "vertex", None),
            P("tm", "vertex", None),
            P("tm", "vertex"),
            P("tm", "vertex", None, None),
            P(),
            P(),
            P(),
            P(),
            P(),
            P(),
            P(),
            P(),
            P(),
        ),
        out_specs=P(None, ("vertex", "tm"), None),
        check_vma=False,
    )
```

```python
import functools

import jax
import jax.numpy as jnp
from jax import lax
from jax.experimental import pallas as pl
from jax.experimental.pallas import tpu as pltpu
from jax.sharding import PartitionSpec as P


TILE = 128
WIDTH = 512
LOCAL = 1024
SLOTS = 128
ROWS = LOCAL // TILE
HALF = LOCAL // 2
STAGES = (
    ((0, 0), (0, 1)),
    ((1, 0), (1, 1), (7, 0), (7, 1)),
    ((2, 0), (2, 1), (6, 0), (6, 1)),
    ((3, 0), (3, 1), (5, 0), (5, 1)),
    ((4, 0),),
    ((4, 1),),
)
LISTS = len(STAGES) + 1
PAIRS = 72
UNROLL = 4
CODES = 2 * LISTS * PAIRS
FFN_PARTS = 4


def in_hbm(array):
    return pltpu.with_memory_space_constraint(array, pltpu.HBM)


def products_kernel(n_bufs, stage, first, last, *refs):
    code_ref, refs = refs[0], refs[1:]
    if first:
        root_ref, refs = refs[0], refs[1:]
    else:
        refs = refs[1:]
    if last:
        base_ref, agg_ref, refs = refs[0], refs[1], refs[2:]
    tiles, bufs, refs = refs[0], refs[1 : 1 + n_bufs], refs[1 + n_bufs :]
    if first:
        acc, base_out, *refs = refs
    elif last:
        acc, out_ref, *refs, out_buf, out_sem = refs
    else:
        acc, *refs = refs
    feat_buf, feat_sem = refs if not last else (None, None)
    start = 0
    feature_copies = []
    for k, buf in enumerate(() if last else bufs):
        copy = pltpu.make_async_copy(
            buf, feat_buf.at[pl.ds(start, buf.shape[0])], feat_sem.at[k]
        )
        copy.start()
        feature_copies.append(copy)
        start += buf.shape[0]
    if first:
        acc[...] = jnp.zeros_like(acc)
    for copy in feature_copies:
        copy.wait()

    def half(code, feats):
        tile = tiles[code & 127]
        live = (code >> 13) & 1
        tile = jnp.where(live == 1, tile, jnp.zeros_like(tile))
        block = pl.multiple_of(((code >> 7) & 63) * TILE, TILE)
        return tile, feats[pl.ds(block, TILE), :]

    for k, feats in enumerate(bufs if last else (feat_buf,)):

        @pl.loop(0, (code_ref[CODES + stage + k] + UNROLL - 1) // UNROLL)
        def _(step, k=k, feats=feats):
            for u in range(UNROLL):
                at = 2 * ((stage + k) * PAIRS + step * UNROLL + u)
                code = code_ref[at]
                tile0, feat0 = half(code, feats)
                tile1, feat1 = half(code_ref[at + 1], feats)
                product = jnp.dot(
                    jnp.concatenate([tile0, tile1], axis=1),
                    jnp.concatenate([feat0, feat1], axis=0),
                    preferred_element_type=jnp.float32,
                )
                rows = pl.ds(pl.multiple_of((code >> 14) * TILE, TILE), TILE)
                acc[rows, :] += product

    if first:

        @pl.loop(0, 4)
        def _(i):
            rows = pl.ds(pl.multiple_of(i * 256, 256), 256)
            base_out[rows, :] = jnp.dot(
                feat_buf[rows, :], root_ref[...], preferred_element_type=jnp.float32
            )

    if last:
        out_copies = []
        for i in range(4):
            rows = slice(i * 256, (i + 1) * 256)
            combined = base_ref[rows, :] + jnp.dot(
                acc[rows, :].astype(jnp.bfloat16),
                agg_ref[...],
                preferred_element_type=jnp.float32,
            )
            out_buf[rows, :] = jax.nn.gelu(combined).astype(jnp.bfloat16)
            span = pl.ds(i * 256, 256)
            copy = pltpu.make_async_copy(out_buf.at[span], out_ref.at[span], out_sem.at[i])
            copy.start()
            out_copies.append(copy)
        for copy in out_copies:
            copy.wait()


def products(stage, codes, extra, tiles, bufs, first=False, last=False):
    n_rows = sum(b.shape[0] for b in bufs)
    smem = pl.BlockSpec(memory_space=pltpu.SMEM)
    vmem = pl.BlockSpec(memory_space=pltpu.VMEM)
    anywhere = pl.BlockSpec(memory_space=pl.ANY)
    scratch = [
        pltpu.VMEM((n_rows, WIDTH), jnp.bfloat16),
        pltpu.SemaphoreType.DMA((len(bufs),)),
    ]
    partial = jax.ShapeDtypeStruct((LOCAL, WIDTH), jnp.float32)
    out, out_specs = partial, vmem
    if first:
        out, out_specs = (partial, partial), (vmem, vmem)
    if last:
        whole = pltpu.HBM((LOCAL, WIDTH), jnp.bfloat16)
        out, out_specs = (partial, whole), (vmem, pl.BlockSpec(memory_space=pltpu.HBM))
        scratch = [
            pltpu.VMEM((LOCAL, WIDTH), jnp.bfloat16),
            pltpu.SemaphoreType.DMA((4,)),
        ]
    return pl.pallas_call(
        functools.partial(products_kernel, len(bufs), stage, first, last),
        out_shape=out,
        in_specs=[smem] + [vmem] * (len(extra) + 1) + [vmem if last else anywhere] * len(bufs),
        out_specs=out_specs,
        scratch_shapes=scratch,
        input_output_aliases={} if first else {1: 0},
        compiler_params=pltpu.CompilerParams(vmem_limit_bytes=16 << 20),
        cost_estimate=pl.CostEstimate(
            flops=2 * LOCAL * n_rows * WIDTH // 4,
            bytes_accessed=n_rows * WIDTH * 2 + (8 << 20),
            transcendentals=0,
        ),
    )(codes, *extra, tiles, *bufs)


def split_kernel(own, low, high, sem):
    copies = [
        pltpu.make_async_copy(own.at[pl.ds(k * HALF, HALF)], out, sem.at[k])
        for k, out in enumerate((low, high))
    ]
    for copy in copies:
        copy.start()
    for copy in copies:
        copy.wait()


def split(own):
    piece = pltpu.VMEM((HALF, WIDTH), jnp.bfloat16)
    vmem = pl.BlockSpec(memory_space=pltpu.VMEM)
    return pl.pallas_call(
        split_kernel,
        out_shape=(piece, piece),
        in_specs=[pl.BlockSpec(memory_space=pltpu.HBM)],
        out_specs=(vmem, vmem),
        scratch_shapes=[pltpu.SemaphoreType.DMA((2,))],
        compiler_params=pltpu.CompilerParams(vmem_limit_bytes=4 << 20),
        name="split",
    )(in_hbm(own))


def norm_rows(values, gain):
    scale = lax.rsqrt(jnp.mean(values * values, axis=-1, keepdims=True) + 1e-06)
    return (values * scale * gain).astype(jnp.bfloat16)


def temporal_kernel(
    rows_ref, embed_ref, gain1_ref, gain2_ref, qkv_ref, out_w_ref, up_hbm, down_hbm, out_ref, *scratch
):
    up_ref, down_ref, out_buf, weight_sem, out_sem = scratch
    late = [
        pltpu.make_async_copy(source, target, weight_sem.at[k])
        for k, (source, target) in enumerate(((up_hbm, up_ref), (down_hbm, down_ref)))
    ]
    for copy in late:
        copy.start()
    items = rows_ref.shape[1]
    groups = items // 8
    embed = embed_ref[...].astype(jnp.float32)
    embed = jnp.broadcast_to(embed[:, None, :], (16, 8, WIDTH)).reshape(TILE, WIDTH)
    values = rows_ref[...].astype(jnp.float32)
    mixed = jnp.concatenate(
        [values[:, g * 8 : (g + 1) * 8, :].reshape(TILE, WIDTH) + embed for g in range(groups)],
        axis=0,
    )
    normed = norm_rows(mixed, gain1_ref[...].astype(jnp.float32))
    qkv = jnp.dot(normed, qkv_ref[...], preferred_element_type=jnp.float32).astype(jnp.bfloat16)

    at = lax.broadcasted_iota(jnp.int32, (2 * TILE, TILE), 0) % TILE
    to = lax.broadcasted_iota(jnp.int32, (2 * TILE, TILE), 1)
    allowed = (at % 8 == to % 8) & (to // 8 <= at // 8)
    lane = lax.broadcasted_iota(jnp.int32, (TILE, TILE), 1)
    low_half = lane < 64
    zero = jnp.zeros((TILE, TILE), jnp.bfloat16)
    one = jnp.ones((TILE, TILE), jnp.bfloat16)
    ones = jnp.concatenate(
        [jnp.where(low_half, one, zero), jnp.where(low_half, zero, one)], axis=0
    )
    contexts = []
    for g in range(groups):
        if g == groups // 2:
            for copy in late:
                copy.wait()
        rows = slice(g * TILE, (g + 1) * TILE)
        pieces = []
        for pair in range(4):
            query = qkv[rows, pair * TILE : (pair + 1) * TILE] * jnp.bfloat16(0.125)
            key = qkv[rows, WIDTH + pair * TILE : WIDTH + (pair + 1) * TILE]
            value = qkv[rows, 2 * WIDTH + pair * TILE : 2 * WIDTH + (pair + 1) * TILE]
            split_query = jnp.concatenate(
                [jnp.where(low_half, query, zero), jnp.where(low_half, zero, query)], axis=0
            )
            split_value = jnp.concatenate(
                [jnp.where(low_half, value, zero), jnp.where(low_half, zero, value)], axis=0
            )
            split_value = jnp.concatenate([split_value, ones], axis=1)
            scores = lax.dot_general(
                split_query, key, (((1,), (1,)), ((), ())), preferred_element_type=jnp.float32
            )
            scores = jnp.where(allowed, scores, -1e30)
            expo = jnp.exp(scores - jnp.max(scores, axis=-1, keepdims=True))
            weights = expo.astype(jnp.bfloat16)
            both = jnp.concatenate([weights[:TILE], weights[TILE:]], axis=1)
            sums = jnp.dot(both, split_value, preferred_element_type=jnp.float32)
            pieces.append(sums[:, :TILE] / sums[:, TILE:])
        contexts.append(jnp.concatenate(pieces, axis=1))
    context = jnp.concatenate(contexts, axis=0).astype(jnp.bfloat16)
    residual = mixed + jnp.dot(context, out_w_ref[...], preferred_element_type=jnp.float32)
    normed_two = norm_rows(residual, gain2_ref[...].astype(jnp.float32))
    count = groups // FFN_PARTS
    out_copies = []
    for part in range(FFN_PARTS):
        rows = slice(part * count * TILE, (part + 1) * count * TILE)
        hidden = jax.nn.gelu(
            jnp.dot(normed_two[rows], up_ref[...], preferred_element_type=jnp.float32)
        ).astype(jnp.bfloat16)
        result = residual[rows] + jnp.dot(
            hidden, down_ref[...], preferred_element_type=jnp.float32
        )
        for k in range(count):
            g = part * count + k
            piece = result[k * TILE : (k + 1) * TILE].reshape(16, 8, WIDTH)
            out_buf[:, g * 8 : (g + 1) * 8, :] = piece.astype(jnp.bfloat16)
        span = pl.ds(part * count * 8, count * 8)
        copy = pltpu.make_async_copy(
            out_buf.at[:, span, :], out_ref.at[:, span, :], out_sem.at[part]
        )
        copy.start()
        out_copies.append(copy)
    for copy in out_copies:
        copy.wait()


def temporal(rows, weights):
    hbm = pl.BlockSpec(memory_space=pltpu.HBM)
    vmem = pl.BlockSpec(memory_space=pltpu.VMEM)
    up, down = (in_hbm(w) for w in weights[-2:])
    return pl.pallas_call(
        temporal_kernel,
        out_shape=jax.ShapeDtypeStruct(rows.shape, jnp.bfloat16),
        in_specs=[vmem] * 6 + [hbm] * 2,
        out_specs=hbm,
        scratch_shapes=[
            pltpu.VMEM(up.shape, up.dtype),
            pltpu.VMEM(down.shape, down.dtype),
            pltpu.VMEM(rows.shape, rows.dtype),
            pltpu.SemaphoreType.DMA((2,)),
            pltpu.SemaphoreType.DMA((FFN_PARTS,)),
        ],
        compiler_params=pltpu.CompilerParams(vmem_limit_bytes=32 << 20),
        name="temporal",
    )(rows, *weights[:-2], up, down)


def plan_kernel(coord_ref, count_ref, out_ref, key_ref, size_ref, next_ref):
    vertex = lax.axis_index("vertex")
    count = count_ref[0, 0]
    n_keys = LISTS * ROWS
    for k in range(n_keys + 1):
        size_ref[k] = 0

    @pl.loop(0, SLOTS, unroll=8)
    def _(slot):
        row, col = coord_ref[0, slot], coord_ref[1, slot]
        distance = ((vertex >> 1) - (col >> 4)) & 7
        other = ((col >> 3) ^ vertex) & 1
        near = jnp.minimum(distance, 8 - distance)
        far = distance == 4
        split_far = jnp.where(far, other, 0)
        stage = near + split_far * (1 + ((col >> 2) & 1))
        block = col & jnp.where(split_far == 1, 3, 7)
        place = jnp.where(far, 0, jnp.where(distance > 4, 2, 0) + other)
        key = jnp.where(slot < count, stage * ROWS + row, n_keys)
        key_ref[slot] = key
        next_ref[slot] = slot + ((place * 8 + block) << 7) + (1 << 13) + (row << 14)
        size_ref[key] = size_ref[key] + 1

    for stage in range(LISTS):
        at = stage * PAIRS
        for key in range(stage * ROWS, (stage + 1) * ROWS):
            size = size_ref[key]
            size_ref[key] = 2 * at
            at = at + ((size + 1) >> 1)
            last = jnp.maximum(at - 1, 0)

            @pl.when((size & 1) == 1)
            def _(last=last):
                out_ref[2 * last + 1] = 0

        out_ref[CODES + stage] = at - stage * PAIRS
        for pad in range(UNROLL - 1):
            out_ref[2 * (at + pad)] = 0
            out_ref[2 * (at + pad) + 1] = 0
    size_ref[n_keys] = CODES + 8

    @pl.loop(0, SLOTS, unroll=8)
    def _(slot):
        key = key_ref[slot]
        at = size_ref[key]
        size_ref[key] = at + 1
        out_ref[at] = next_ref[slot]


def plan(pairs, count):
    smem = pl.BlockSpec(memory_space=pltpu.SMEM)
    return pl.pallas_call(
        plan_kernel,
        out_shape=jax.ShapeDtypeStruct((CODES + 8 + SLOTS,), jnp.int32),
        in_specs=[smem, smem],
        out_specs=smem,
        scratch_shapes=[pltpu.SMEM((SLOTS,), jnp.int32)] * 3,
        compiler_params=pltpu.CompilerParams(vmem_limit_bytes=1 << 20),
        cost_estimate=pl.CostEstimate(flops=1 << 20, bytes_accessed=1 << 20, transcendentals=0),
        name="plan",
    )(pairs.T, count)


def layer(
    features,
    tile_coord,
    tile_count,
    tile_values,
    w_agg,
    w_root,
    time_embed,
    gain_first,
    w_qkv,
    w_out,
    gain_second,
    w_up,
    w_down,
):
    own = features[0]
    tiles = tile_values[0]
    n_vertex = lax.axis_size("vertex")

    def hop(x, step):
        return lax.ppermute(x, "vertex", [(v, (v + 2 * step) % n_vertex) for v in range(n_vertex)])

    def swap(x):
        return lax.ppermute(x, "vertex", [(v, v ^ 1) for v in range(n_vertex)])

    chunks = split(own)
    got = {(0, 0): (in_hbm(own),), (0, 1): (swap(own),)}
    right, left = list(chunks), list(chunks)
    for h in (1, 2, 3, 4):
        if h < 4:
            right = [hop(right[c], 1) for c in (0, 1)]
            left = [hop(left[c], -1) for c in (0, 1)]
            got[h, 0], got[8 - h, 0] = right, left
            got[h, 1] = [swap(right[c]) for c in (0, 1)]
            got[8 - h, 1] = [swap(left[c]) for c in (0, 1)]
        else:
            far = (hop(right[0], 1), hop(left[1], -1))
            got[4, 0] = far
            got[4, 1] = (swap(far[0]), swap(far[1]))

    codes = plan(tile_coord[0], tile_count)
    bufs = [[b for source in sources for b in got[source]] for sources in STAGES]
    acc, base = products(0, codes, (w_root,), tiles, bufs[0], first=True)
    for s in range(1, len(STAGES) - 1):
        acc = products(s, codes, (acc,), tiles, bufs[s])
    s = len(STAGES) - 1
    rows = products(s, codes, (acc, base, w_agg), tiles, bufs[s], last=True)[1]
    tm_count = lax.axis_size("tm")
    sections = rows.reshape(tm_count, LOCAL // tm_count, WIDTH)
    arrived = lax.all_to_all(sections, "tm", split_axis=0, concat_axis=0, tiled=True)
    weights = (time_embed, gain_first[None, :], gain_second[None, :])
    weights += (w_qkv, w_out, w_up, w_down)
    return temporal(arrived, weights)


def solution(mesh):
    return jax.shard_map(
        layer,
        mesh=mesh,
        in_specs=(
            P("tm", "vertex", None),
            P("tm", "vertex", None),
            P("tm", "vertex"),
            P("tm", "vertex", None, None),
            P(),
            P(),
            P(),
            P(),
            P(),
            P(),
            P(),
            P(),
            P(),
        ),
        out_specs=P(None, ("vertex", "tm"), None),
        check_vma=False,
    )
```

```python
import functools

import jax
import jax.numpy as jnp
from jax import lax
from jax.experimental import pallas as pl
from jax.experimental.pallas import tpu as pltpu
from jax.sharding import PartitionSpec as P


TILE = 128
WIDTH = 512
LOCAL = 1024
SLOTS = 128
ROWS = LOCAL // TILE
HALF = LOCAL // 2
STAGES = (
    ((0, 0), (0, 1)),
    ((1, 0), (1, 1), (7, 0), (7, 1)),
    ((2, 0), (2, 1), (6, 0), (6, 1)),
    ((3, 0), (3, 1), (5, 0), (5, 1)),
    ((4, 0),),
    ((4, 1),),
)
LISTS = len(STAGES) + 1
PAIRS = 72
UNROLL = 4
CODES = 2 * LISTS * PAIRS
FFN_PARTS = 4


def in_hbm(array):
    return pltpu.with_memory_space_constraint(array, pltpu.HBM)


def products_kernel(n_bufs, stage, first, last, *refs):
    code_ref, refs = refs[0], refs[1:]
    if first:
        root_ref, refs = refs[0], refs[1:]
    else:
        refs = refs[1:]
    if last:
        base_ref, agg_ref, refs = refs[0], refs[1], refs[2:]
    tiles, bufs, refs = refs[0], refs[1 : 1 + n_bufs], refs[1 + n_bufs :]
    if first:
        acc, base_out, *refs = refs
    elif last:
        acc, out_ref, *refs, out_buf, out_sem = refs
    else:
        acc, *refs = refs
    feat_buf, feat_sem = refs if not last else (None, None)
    start = 0
    feature_copies = []
    for k, buf in enumerate(() if last else bufs):
        copy = pltpu.make_async_copy(
            buf, feat_buf.at[pl.ds(start, buf.shape[0])], feat_sem.at[k]
        )
        copy.start()
        feature_copies.append(copy)
        start += buf.shape[0]
    if first:
        acc[...] = jnp.zeros_like(acc)
    for copy in feature_copies:
        copy.wait()

    def half(code, feats):
        tile = tiles[code & 127]
        live = (code >> 13) & 1
        tile = jnp.where(live == 1, tile, jnp.zeros_like(tile))
        block = pl.multiple_of(((code >> 7) & 63) * TILE, TILE)
        return tile, feats[pl.ds(block, TILE), :]

    unroll = 2 if last else UNROLL
    for k, feats in enumerate(bufs if last else (feat_buf,)):

        @pl.loop(0, (code_ref[CODES + stage + k] + unroll - 1) // unroll)
        def _(step, k=k, feats=feats):
            for u in range(unroll):
                at = 2 * ((stage + k) * PAIRS + step * unroll + u)
                code = code_ref[at]
                tile0, feat0 = half(code, feats)
                tile1, feat1 = half(code_ref[at + 1], feats)
                product = jnp.dot(
                    jnp.concatenate([tile0, tile1], axis=1),
                    jnp.concatenate([feat0, feat1], axis=0),
                    preferred_element_type=jnp.float32,
                )
                rows = pl.ds(pl.multiple_of((code >> 14) * TILE, TILE), TILE)
                acc[rows, :] += product

    if first:

        @pl.loop(0, 4)
        def _(i):
            rows = pl.ds(pl.multiple_of(i * 256, 256), 256)
            base_out[rows, :] = jnp.dot(
                feat_buf[rows, :], root_ref[...], preferred_element_type=jnp.float32
            )

    if last:
        out_copies = []
        for i in range(4):
            rows = slice(i * 256, (i + 1) * 256)
            combined = base_ref[rows, :] + jnp.dot(
                acc[rows, :].astype(jnp.bfloat16),
                agg_ref[...],
                preferred_element_type=jnp.float32,
            )
            out_buf[rows, :] = jax.nn.gelu(combined).astype(jnp.bfloat16)
            span = pl.ds(i * 256, 256)
            copy = pltpu.make_async_copy(out_buf.at[span], out_ref.at[span], out_sem.at[i])
            copy.start()
            out_copies.append(copy)
        for copy in out_copies:
            copy.wait()


def products(stage, codes, extra, tiles, bufs, first=False, last=False):
    n_rows = sum(b.shape[0] for b in bufs)
    smem = pl.BlockSpec(memory_space=pltpu.SMEM)
    vmem = pl.BlockSpec(memory_space=pltpu.VMEM)
    anywhere = pl.BlockSpec(memory_space=pl.ANY)
    scratch = [
        pltpu.VMEM((n_rows, WIDTH), jnp.bfloat16),
        pltpu.SemaphoreType.DMA((len(bufs),)),
    ]
    partial = jax.ShapeDtypeStruct((LOCAL, WIDTH), jnp.float32)
    out, out_specs = partial, vmem
    if first:
        out, out_specs = (partial, partial), (vmem, vmem)
    if last:
        whole = pltpu.HBM((LOCAL, WIDTH), jnp.bfloat16)
        out, out_specs = (partial, whole), (vmem, pl.BlockSpec(memory_space=pltpu.HBM))
        scratch = [
            pltpu.VMEM((LOCAL, WIDTH), jnp.bfloat16),
            pltpu.SemaphoreType.DMA((4,)),
        ]
    return pl.pallas_call(
        functools.partial(products_kernel, len(bufs), stage, first, last),
        out_shape=out,
        in_specs=[smem] + [vmem] * (len(extra) + 1) + [vmem if last else anywhere] * len(bufs),
        out_specs=out_specs,
        scratch_shapes=scratch,
        input_output_aliases={} if first else {1: 0},
        compiler_params=pltpu.CompilerParams(vmem_limit_bytes=16 << 20),
        cost_estimate=pl.CostEstimate(
            flops=2 * LOCAL * n_rows * WIDTH // 4,
            bytes_accessed=n_rows * WIDTH * 2 + (8 << 20),
            transcendentals=0,
        ),
    )(codes, *extra, tiles, *bufs)


def split_kernel(own, low, high, sem):
    copies = [
        pltpu.make_async_copy(own.at[pl.ds(k * HALF, HALF)], out, sem.at[k])
        for k, out in enumerate((low, high))
    ]
    for copy in copies:
        copy.start()
    for copy in copies:
        copy.wait()


def split(own):
    piece = pltpu.VMEM((HALF, WIDTH), jnp.bfloat16)
    vmem = pl.BlockSpec(memory_space=pltpu.VMEM)
    return pl.pallas_call(
        split_kernel,
        out_shape=(piece, piece),
        in_specs=[pl.BlockSpec(memory_space=pltpu.HBM)],
        out_specs=(vmem, vmem),
        scratch_shapes=[pltpu.SemaphoreType.DMA((2,))],
        compiler_params=pltpu.CompilerParams(vmem_limit_bytes=4 << 20),
        name="split",
    )(in_hbm(own))


def norm_rows(values, gain):
    scale = lax.rsqrt(jnp.mean(values * values, axis=-1, keepdims=True) + 1e-06)
    return (values * scale * gain).astype(jnp.bfloat16)


def temporal_kernel(
    rows_ref, embed_ref, gain1_ref, gain2_ref, qkv_ref, out_w_ref, up_hbm, down_hbm, out_ref, *scratch
):
    up_ref, down_ref, out_buf, weight_sem, out_sem = scratch
    late = [
        pltpu.make_async_copy(source, target, weight_sem.at[k])
        for k, (source, target) in enumerate(((up_hbm, up_ref), (down_hbm, down_ref)))
    ]
    for copy in late:
        copy.start()
    items = rows_ref.shape[1]
    groups = items // 8
    embed = embed_ref[...].astype(jnp.float32)
    embed = jnp.broadcast_to(embed[:, None, :], (16, 8, WIDTH)).reshape(TILE, WIDTH)
    values = rows_ref[...].astype(jnp.float32)
    mixed = jnp.concatenate(
        [values[:, g * 8 : (g + 1) * 8, :].reshape(TILE, WIDTH) + embed for g in range(groups)],
        axis=0,
    )
    normed = norm_rows(mixed, gain1_ref[...].astype(jnp.float32))
    qkv = jnp.dot(normed, qkv_ref[...], preferred_element_type=jnp.float32).astype(jnp.bfloat16)

    at = lax.broadcasted_iota(jnp.int32, (2 * TILE, TILE), 0) % TILE
    to = lax.broadcasted_iota(jnp.int32, (2 * TILE, TILE), 1)
    allowed = (at % 8 == to % 8) & (to // 8 <= at // 8)
    lane = lax.broadcasted_iota(jnp.int32, (TILE, TILE), 1)
    low_half = lane < 64
    zero = jnp.zeros((TILE, TILE), jnp.bfloat16)
    one = jnp.ones((TILE, TILE), jnp.bfloat16)
    ones = jnp.concatenate(
        [jnp.where(low_half, one, zero), jnp.where(low_half, zero, one)], axis=0
    )
    contexts = []
    for g in range(groups):
        if g == groups // 2:
            for copy in late:
                copy.wait()
        rows = slice(g * TILE, (g + 1) * TILE)
        pieces = []
        for pair in range(4):
            query = qkv[rows, pair * TILE : (pair + 1) * TILE] * jnp.bfloat16(0.125)
            key = qkv[rows, WIDTH + pair * TILE : WIDTH + (pair + 1) * TILE]
            value = qkv[rows, 2 * WIDTH + pair * TILE : 2 * WIDTH + (pair + 1) * TILE]
            split_query = jnp.concatenate(
                [jnp.where(low_half, query, zero), jnp.where(low_half, zero, query)], axis=0
            )
            split_value = jnp.concatenate(
                [jnp.where(low_half, value, zero), jnp.where(low_half, zero, value)], axis=0
            )
            split_value = jnp.concatenate([split_value, ones], axis=1)
            scores = lax.dot_general(
                split_query, key, (((1,), (1,)), ((), ())), preferred_element_type=jnp.float32
            )
            scores = jnp.where(allowed, scores, -1e30)
            expo = jnp.exp(scores - jnp.max(scores, axis=-1, keepdims=True))
            weights = expo.astype(jnp.bfloat16)
            both = jnp.concatenate([weights[:TILE], weights[TILE:]], axis=1)
            sums = jnp.dot(both, split_value, preferred_element_type=jnp.float32)
            pieces.append(sums[:, :TILE] / sums[:, TILE:])
        contexts.append(jnp.concatenate(pieces, axis=1))
    context = jnp.concatenate(contexts, axis=0).astype(jnp.bfloat16)
    residual = mixed + jnp.dot(context, out_w_ref[...], preferred_element_type=jnp.float32)
    normed_two = norm_rows(residual, gain2_ref[...].astype(jnp.float32))
    count = groups // FFN_PARTS
    out_copies = []
    for part in range(FFN_PARTS):
        rows = slice(part * count * TILE, (part + 1) * count * TILE)
        hidden = jax.nn.gelu(
            jnp.dot(normed_two[rows], up_ref[...], preferred_element_type=jnp.float32)
        ).astype(jnp.bfloat16)
        result = residual[rows] + jnp.dot(
            hidden, down_ref[...], preferred_element_type=jnp.float32
        )
        for k in range(count):
            g = part * count + k
            piece = result[k * TILE : (k + 1) * TILE].reshape(16, 8, WIDTH)
            out_buf[:, g * 8 : (g + 1) * 8, :] = piece.astype(jnp.bfloat16)
        span = pl.ds(part * count * 8, count * 8)
        copy = pltpu.make_async_copy(
            out_buf.at[:, span, :], out_ref.at[:, span, :], out_sem.at[part]
        )
        copy.start()
        out_copies.append(copy)
    for copy in out_copies:
        copy.wait()


def temporal(rows, weights):
    hbm = pl.BlockSpec(memory_space=pltpu.HBM)
    vmem = pl.BlockSpec(memory_space=pltpu.VMEM)
    up, down = (in_hbm(w) for w in weights[-2:])
    return pl.pallas_call(
        temporal_kernel,
        out_shape=jax.ShapeDtypeStruct(rows.shape, jnp.bfloat16),
        in_specs=[vmem] * 6 + [hbm] * 2,
        out_specs=hbm,
        scratch_shapes=[
            pltpu.VMEM(up.shape, up.dtype),
            pltpu.VMEM(down.shape, down.dtype),
            pltpu.VMEM(rows.shape, rows.dtype),
            pltpu.SemaphoreType.DMA((2,)),
            pltpu.SemaphoreType.DMA((FFN_PARTS,)),
        ],
        compiler_params=pltpu.CompilerParams(vmem_limit_bytes=32 << 20),
        name="temporal",
    )(rows, *weights[:-2], up, down)


def plan_kernel(coord_ref, count_ref, out_ref, key_ref, size_ref, next_ref):
    vertex = lax.axis_index("vertex")
    count = count_ref[0, 0]
    n_keys = LISTS * ROWS
    for k in range(n_keys + 1):
        size_ref[k] = 0

    @pl.loop(0, SLOTS, unroll=8)
    def _(slot):
        row, col = coord_ref[0, slot], coord_ref[1, slot]
        distance = ((vertex >> 1) - (col >> 4)) & 7
        other = ((col >> 3) ^ vertex) & 1
        near = jnp.minimum(distance, 8 - distance)
        far = distance == 4
        split_far = jnp.where(far, other, 0)
        stage = near + split_far * (1 + ((col >> 2) & 1))
        block = col & jnp.where(split_far == 1, 3, 7)
        place = jnp.where(far, 0, jnp.where(distance > 4, 2, 0) + other)
        key = jnp.where(slot < count, stage * ROWS + row, n_keys)
        key_ref[slot] = key
        next_ref[slot] = slot + ((place * 8 + block) << 7) + (1 << 13) + (row << 14)
        size_ref[key] = size_ref[key] + 1

    for stage in range(LISTS):
        at = stage * PAIRS
        for key in range(stage * ROWS, (stage + 1) * ROWS):
            size = size_ref[key]
            size_ref[key] = 2 * at
            at = at + ((size + 1) >> 1)
            last = jnp.maximum(at - 1, 0)

            @pl.when((size & 1) == 1)
            def _(last=last):
                out_ref[2 * last + 1] = 0

        out_ref[CODES + stage] = at - stage * PAIRS
        for pad in range(UNROLL - 1):
            out_ref[2 * (at + pad)] = 0
            out_ref[2 * (at + pad) + 1] = 0
    size_ref[n_keys] = CODES + 8

    @pl.loop(0, SLOTS, unroll=8)
    def _(slot):
        key = key_ref[slot]
        at = size_ref[key]
        size_ref[key] = at + 1
        out_ref[at] = next_ref[slot]


def plan(pairs, count):
    smem = pl.BlockSpec(memory_space=pltpu.SMEM)
    return pl.pallas_call(
        plan_kernel,
        out_shape=jax.ShapeDtypeStruct((CODES + 8 + SLOTS,), jnp.int32),
        in_specs=[smem, smem],
        out_specs=smem,
        scratch_shapes=[pltpu.SMEM((SLOTS,), jnp.int32)] * 3,
        compiler_params=pltpu.CompilerParams(vmem_limit_bytes=1 << 20),
        cost_estimate=pl.CostEstimate(flops=1 << 20, bytes_accessed=1 << 20, transcendentals=0),
        name="plan",
    )(pairs.T, count)


def layer(
    features,
    tile_coord,
    tile_count,
    tile_values,
    w_agg,
    w_root,
    time_embed,
    gain_first,
    w_qkv,
    w_out,
    gain_second,
    w_up,
    w_down,
):
    own = features[0]
    tiles = tile_values[0]
    n_vertex = lax.axis_size("vertex")

    def hop(x, step):
        return lax.ppermute(x, "vertex", [(v, (v + 2 * step) % n_vertex) for v in range(n_vertex)])

    def swap(x):
        return lax.ppermute(x, "vertex", [(v, v ^ 1) for v in range(n_vertex)])

    chunks = split(own)
    got = {(0, 0): (in_hbm(own),), (0, 1): (swap(own),)}
    right, left = list(chunks), list(chunks)
    for h in (1, 2, 3, 4):
        if h < 4:
            right = [hop(right[c], 1) for c in (0, 1)]
            left = [hop(left[c], -1) for c in (0, 1)]
            got[h, 0], got[8 - h, 0] = right, left
            got[h, 1] = [swap(right[c]) for c in (0, 1)]
            got[8 - h, 1] = [swap(left[c]) for c in (0, 1)]
        else:
            far = (hop(right[0], 1), hop(left[1], -1))
            got[4, 0] = far
            got[4, 1] = (swap(far[0]), swap(far[1]))

    codes = plan(tile_coord[0], tile_count)
    bufs = [[b for source in sources for b in got[source]] for sources in STAGES]
    acc, base = products(0, codes, (w_root,), tiles, bufs[0], first=True)
    for s in range(1, len(STAGES) - 1):
        acc = products(s, codes, (acc,), tiles, bufs[s])
    s = len(STAGES) - 1
    rows = products(s, codes, (acc, base, w_agg), tiles, bufs[s], last=True)[1]
    tm_count = lax.axis_size("tm")
    sections = rows.reshape(tm_count, LOCAL // tm_count, WIDTH)
    arrived = lax.all_to_all(sections, "tm", split_axis=0, concat_axis=0, tiled=True)
    weights = (time_embed, gain_first[None, :], gain_second[None, :])
    weights += (w_qkv, w_out, w_up, w_down)
    return temporal(arrived, weights)


def solution(mesh):
    return jax.shard_map(
        layer,
        mesh=mesh,
        in_specs=(
            P("tm", "vertex", None),
            P("tm", "vertex", None),
            P("tm", "vertex"),
            P("tm", "vertex", None, None),
            P(),
            P(),
            P(),
            P(),
            P(),
            P(),
            P(),
            P(),
            P(),
        ),
        out_specs=P(None, ("vertex", "tm"), None),
        check_vma=False,
    )
```
